32 devices in a mesh: src: 16 (over z, x, core), tgt: 2 (over y).
Axes of the slice: x: 2, y: 2, z: 4, core: 2. Of those that a mesh axis runs over, the one named last changes fastest.
Arguments:
- source_embed: bfloat16 [128, 65536], P(None, 'src'), may hold values from -1 to 1
- target_embed: bfloat16 [128, 1024], P(None, 'tgt'), may hold values from -1 to 1
- source_expr: bfloat16 [128, 65536], P(None, 'src'), may hold values from -0.5390625 to 0.5390625
- target_expr: bfloat16 [128, 1024], P(None, 'tgt'), may hold values from -0.5390625 to 0.5390625
- current_plan: bfloat16 [65536, 1024], P('src', 'tgt'), as said below
- source_mass: float32 [65536], P('src'), may hold values from 0.25 to 4
- target_mass: float32 [1024], P('tgt'), may hold values from 0.25 to 4
- source_potential: float32 [65536], P('src'), may hold values from -16 to 16
- target_genes: bfloat16 [1024, 256], P('tgt'), may hold values from -6 to 6
Outputs:
- imputed: bfloat16 [65536, 256], P(('src', 'tgt'))
The draws below stay inside these ranges and needn't reach their ends.
Inputs may be any that keep to these rules, and one draw needn't show every extreme that they name: Every entry of current_plan is positive.
All inputs are finite; a program needn't handle non-finite values.
Results may differ from the reference program's by a relative error of at most 0.014.
Values may be sent and summed in bfloat16 or wider, within the bound.
A program may use at most 64 MiB of HBM per device.

```python
import math
import jax
import jax.numpy as jnp
from jax import lax

D = 128
GENES = 256
ITERS = 2
RANK = 130
NS = 65536
NT = 1024


group_count = 256


def cluster_labels(key, amount, salt_value):
    return jax.random.randint(jax.random.fold_in(key, salt_value), (amount,), 0, group_count)


def embed_spots(key, labels, salt_value):
    centres = jax.random.normal(jax.random.fold_in(key, 101), (D, group_count), jnp.float32) * 0.075
    placed = jnp.take(centres, labels, axis=1)
    amount = labels.shape[0]
    values = placed + 0.05 * jax.random.normal(jax.random.fold_in(key, salt_value), (D, amount), jnp.float32)
    return jnp.clip(values, -1.0, 1.0).astype(jnp.bfloat16)


def draw_source_embed(key, part):
    return embed_spots(key, cluster_labels(key, NS, 202), 11)


def draw_target_embed(key, part):
    return embed_spots(key, cluster_labels(key, NT, 303), 21)


def draw_current_plan(key, part):
    label_src = cluster_labels(key, NS, 202)
    label_tgt = cluster_labels(key, NT, 303)
    matched = (label_src[:, None] == label_tgt[None, :]).astype(jnp.float32)
    rising = 0.5 + (jnp.arange(NS, dtype=jnp.float32) + 0.5) / NS
    jitter = jnp.exp(0.5 * jnp.clip(jax.random.normal(jax.random.fold_in(key, 404), (NS, NT), jnp.float32), -6.0, 6.0))
    entries = jitter * (1.0 + 1024.0 * matched) * rising[:, None] / 5.67
    return entries.astype(jnp.bfloat16)


def draw_source_potential(key, part):
    base = 0.1 * jnp.clip(jax.random.normal(jax.random.fold_in(key, 505), (NS,), jnp.float32), -4.0, 4.0)
    group_level = jnp.exp(jax.random.uniform(jax.random.fold_in(key, 606), (NS // 32,), jnp.float32, math.log(4.0), math.log(14.0)))
    tie_gap = jax.random.uniform(jax.random.fold_in(key, 707), (NS // 32,), jnp.float32, 0.05, 0.15)
    position = jnp.arange(NS, dtype=jnp.int32) % 32
    level = jnp.repeat(group_level, 32)
    gap = jnp.repeat(tie_gap, 32)
    first = (position == 3).astype(jnp.float32)
    second = (position == 4).astype(jnp.float32)
    bumped = first * level + second * (level + gap)
    return base * (1.0 - first - second) + bumped


def block_scale(key, shape, shards, smallest, top_value):
    def one(axis_at, blocks):
        steps = jax.random.uniform(jax.random.fold_in(jax.random.fold_in(key, 6), axis_at), (blocks,), jnp.float32, smallest / len(shards), top_value / len(shards))
        return jnp.repeat(jnp.exp(steps), shape[axis_at] // blocks).reshape((-1,) + (1,) * (len(shape) - axis_at - 1))

    gain = one(*shards[0])
    for cut in shards[1:]:
        gain = gain * one(*cut)
    return gain


def bell_draw(stream_key, shape, width, bound, split=(), held_as=jnp.bfloat16):
    values = jax.random.normal(stream_key, shape, jnp.float32) * width
    if len(split) > 0:
        values = block_scale(stream_key, shape, split, -0.22, 0.18) * values
    return jnp.clip(values, min=-bound, max=bound).astype(held_as)


def setup_inputs(seed: int = 0) -> dict:
    keys = jax.random.split(jax.random.key(seed), 10)
    source_embed = draw_source_embed(jax.random.fold_in(keys[9], 71), 0)
    target_embed = draw_target_embed(jax.random.fold_in(keys[9], 71), 0)
    source_expr = bell_draw(keys[2], (D, NS), 0.09, 0.5390625, ((1, 16),))
    target_expr = bell_draw(keys[3], (D, NT), 0.09, 0.5390625, ((1, 2),))
    current_plan = draw_current_plan(jax.random.fold_in(keys[9], 71), 0)
    source_mass = jnp.clip(jnp.exp(math.log(4.0) - 2.7725887 * jax.random.uniform(keys[5], (NS,), jnp.float32) ** block_scale(keys[5], (NS,), ((0, 16),), -0.2, 0.2)), 0.25, 4.0)
    target_mass = jnp.clip(jnp.exp(math.log(4.0) - 2.7725887 * jax.random.uniform(keys[6], (NT,), jnp.float32) ** block_scale(keys[6], (NT,), ((0, 2),), -0.2, 0.2)), 0.25, 4.0)
    source_potential = draw_source_potential(jax.random.fold_in(keys[9], 71), 0)
    target_genes = bell_draw(keys[8], (NT, GENES), 1.0, 6.0, ((0, 2),))
    return dict(source_embed=source_embed, target_embed=target_embed, source_expr=source_expr, target_expr=target_expr, current_plan=current_plan, source_mass=source_mass, target_mass=target_mass, source_potential=source_potential, target_genes=target_genes)


epsilon = 0.05
geometry_weight = 4.0


def factors(embed):
    widened = embed.astype(jnp.float32)
    squares = jnp.sum(widened * widened, axis=0)
    unit_row = jnp.ones_like(squares)
    left_factor = jnp.concatenate([squares[None, :], unit_row[None, :], -2.0 * widened], axis=0)
    right_factor = jnp.concatenate([unit_row[None, :], squares[None, :], widened], axis=0)
    return left_factor, right_factor


def reference(source_embed, target_embed, source_expr, target_expr, current_plan, source_mass, target_mass, source_potential, target_genes):
    highest = lax.Precision.HIGHEST
    block_rows = math.gcd(NS, 2048)
    block_count = NS // block_rows
    left_src, right_src = factors(source_embed)
    left_tgt, right_tgt = factors(target_embed)
    plan_blocks = current_plan.reshape(block_count, block_rows, NT)

    def core_rows(plan_block):
        return jnp.dot(plan_block.astype(jnp.float32), right_tgt.T, precision=highest, preferred_element_type=jnp.float32)

    projected = lax.map(core_rows, plan_blocks).reshape(NS, RANK)
    core_matrix = jnp.dot(right_src, projected, precision=highest, preferred_element_type=jnp.float32) / (NS * NT)
    geometry_right = jnp.dot(core_matrix, left_tgt, precision=highest, preferred_element_type=jnp.float32)

    def cost_block(block_index):
        offset = (block_index * block_rows).astype(jnp.int32)
        expr_block = lax.dynamic_slice_in_dim(source_expr, offset, block_rows, 1)
        factor_block = lax.dynamic_slice_in_dim(left_src, offset, block_rows, 1)
        feature = jnp.dot(expr_block.T, target_expr, preferred_element_type=jnp.float32)
        geometry = jnp.dot(factor_block.T, geometry_right, precision=highest, preferred_element_type=jnp.float32)
        return -2.0 * (feature + geometry_weight * geometry)

    cost_tiles = lax.map(cost_block, jnp.arange(block_count, dtype=jnp.int32))
    log_src = jnp.log(source_mass).reshape(block_count, block_rows)
    log_tgt = jnp.log(target_mass)
    potential_src = source_potential.reshape(block_count, block_rows)
    potential_tgt = jnp.zeros((NT,), jnp.float32)
    for iteration in range(ITERS):
        def column_step(carry_pair, inputs):
            running_max, running_sum = carry_pair
            cost_piece, potential_piece = inputs
            scores = (potential_piece[:, None] - cost_piece) / epsilon
            maximum = jnp.maximum(running_max, jnp.max(scores, axis=0))
            running_sum = running_sum * jnp.exp(running_max - maximum) + jnp.sum(jnp.exp(scores - maximum[None, :]), axis=0)
            return (maximum, running_sum), None

        start_max = jnp.full((NT,), -jnp.inf, dtype=jnp.float32)
        start_sum = jnp.zeros((NT,), jnp.float32)
        (column_max, column_sum), unused = lax.scan(column_step, (start_max, start_sum), (cost_tiles, potential_src))
        potential_tgt = epsilon * log_tgt - epsilon * (column_max + jnp.log(column_sum))

        def row_step(cost_piece, current_tgt=potential_tgt):
            scores = (current_tgt[None, :] - cost_piece) / epsilon
            maximum = jnp.max(scores, axis=1)
            return maximum + jnp.log(jnp.sum(jnp.exp(scores - maximum[:, None]), axis=1))

        potential_src = epsilon * log_src - epsilon * lax.map(row_step, cost_tiles)

    def impute_block(pieces):
        cost_piece, potential_piece, mass_piece = pieces
        weights = jnp.exp((potential_piece[:, None] + potential_tgt[None, :] - cost_piece) / epsilon).astype(jnp.bfloat16)
        return jnp.dot(weights, target_genes, preferred_element_type=jnp.float32) / mass_piece[:, None]

    imputed = lax.map(impute_block, (cost_tiles, potential_src, source_mass.reshape(block_count, block_rows)))
    return imputed.reshape(NS, GENES).astype(jnp.bfloat16)
```

```python
import functools
import math

import jax
import jax.numpy as jnp
from jax import lax
from jax.experimental import pallas as pl
from jax.experimental.pallas import tpu as pltpu
from jax.sharding import PartitionSpec as P

EPSILON = 0.05
GEOMETRY_WEIGHT = 4.0
LOG2E = math.log2(math.e)
KAPPA = 2.0 * LOG2E / EPSILON
MESH = pl.DeviceIdType.MESH
F32 = jnp.float32
BF16 = jnp.bfloat16
TILES = 17
CHUNKS = 4


def split3(value):
    high = value.astype(BF16)
    rest = value - high.astype(F32)
    middle = rest.astype(BF16)
    low = (rest - middle.astype(F32)).astype(BF16)
    return high, middle, low


def dot(a, b, dims=((1,), (0,))):
    return lax.dot_general(a, b, (dims, ((), ())), preferred_element_type=F32)


def dot3(a, b, dims=((1,), (0,))):
    high, middle, low = split3(a)
    return dot(high, b, dims) + (dot(middle, b, dims) + dot(low, b, dims))


def rows_of(count, width, values):
    row = lax.broadcasted_iota(jnp.int32, (count, width), 0)
    held = jnp.zeros((count, width), F32)
    for k, value in enumerate(values):
        held = jnp.where(row == k, value, held)
    return held


def kernel(
    src_n, tgt_n, total_pairs, rows, score_step, middle_step, last_step,
    es_ref, et_ref, xs_ref, xt_ref, plan_ref, ms_ref, mt_ref, fs_ref, genes_ref,
    out_ref,
    right, plan, xs, emb, expr, tmass, genes, partial, collected, core,
    border, lhs, mass, rhs, score, prob, weighted, slots, gpot, colmax, colsum,
    in_sem, tgt_send, tgt_recv, fw_send, fw_recv, rs_send, rs_recv, ag_send, ag_recv,
    col_send, col_recv,
):
    n = src_n * tgt_n
    s = lax.axis_index("src")
    t = lax.axis_index("tgt")
    me = s * tgt_n + t
    cols = et_ref.shape[1]
    nt = cols * tgt_n
    local = es_ref.shape[1]
    lanes = nt // 128
    gene_count = genes_ref.shape[1]
    base = t * rows

    def place(linear):
        return (linear // tgt_n, linear % tgt_n)

    def distant(h):
        return n // 2 + (1 - 2 * (h % 2)) * ((h + 1) // 2)

    def owner(tile):
        if tile < 16:
            return (src_n // 2 - 4 + tile // 2, (tile % 2) * (tgt_n // 2))
        return (src_n // 2 + 4, 0)

    barrier = pltpu.get_barrier_semaphore()

    def greet(h, carry):
        pl.semaphore_signal(
            barrier, inc=1, device_id=place((me + distant(h)) % n), device_id_type=MESH
        )
        return carry

    lax.fori_loop(0, n - 1, greet, 0)

    plan_step = local // CHUNKS
    fetch_embed = pltpu.make_async_copy(es_ref, right.at[0:128], in_sem.at[0])
    fetch_plan = [
        pltpu.make_async_copy(
            plan_ref.at[c * plan_step:(c + 1) * plan_step],
            plan.at[c * plan_step:(c + 1) * plan_step], in_sem.at[3 + c],
        )
        for c in range(CHUNKS)
    ]
    fetch_expr = pltpu.make_async_copy(
        xs_ref.at[:, pl.ds(pl.multiple_of(base, 128), rows)], xs, in_sem.at[1]
    )
    fetch_genes = pltpu.make_async_copy(genes_ref, genes.at[t], in_sem.at[2])
    for copy in [fetch_embed] + fetch_plan + [fetch_expr, fetch_genes]:
        copy.start()
    emb[t] = et_ref[...]
    expr[t] = xt_ref[...]
    tmass[t] = mt_ref[...]
    target = et_ref[...]
    target_wide = target.astype(F32)
    q_tgt = [p.astype(F32) for p in split3(jnp.sum(target_wide * target_wide, axis=0, keepdims=True))]
    fetch_embed.wait()

    wide = right[0:128, :].astype(F32)
    q_src = [p.astype(F32) for p in split3(jnp.sum(wide * wide, axis=0, keepdims=True))]
    right[128:144, :] = rows_of(16, local, [1.0] + q_src).astype(BF16)

    here = 0.0
    for c in range(CHUNKS):
        fetch_plan[c].wait()
        at = slice(c * plan_step, (c + 1) * plan_step)
        here = here + dot(right[:, at], plan[at, :])
    by_e = here[0:128, :]
    by_one = here[128:129, :]
    by_q = here[129:130, :] + (here[130:131, :] + here[131:132, :])
    high, mid, low = split3(by_e)
    across_dims = ((1,), (1,))
    partial[0:16] = (
        dot(high, target, across_dims) + (dot(mid, target, across_dims) + dot(low, target, across_dims))
    ).reshape(16, 8, 128)
    ends = rows_of(16, cols, [1.0] + q_tgt).astype(BF16)
    ends = dot(ends, high, across_dims) + (dot(ends, mid, across_dims) + dot(ends, low, across_dims))
    q_wide = q_tgt[0] + (q_tgt[1] + q_tgt[2])
    row = lax.broadcasted_iota(jnp.int32, (8, 128), 0)
    edge_t = jnp.where(row == 0, ends[0:1, :], jnp.where(row == 1, ends[1:2, :] + (ends[2:3, :] + ends[3:4, :]), 0.0))
    sums = rows_of(8, cols, [0.0, 0.0, by_one, by_q])
    scalars = rows_of(8, cols, [0.0, 0.0, 0.0, 0.0, by_one, by_one * q_wide, by_q, by_q * q_wide])
    partial[16] = edge_t + dot3(sums, target, across_dims) + jnp.sum(scalars, axis=1, keepdims=True)

    pl.semaphore_wait(barrier, n - 1)

    def to_owner(tile):
        return pltpu.make_async_remote_copy(
            src_ref=partial.at[tile], dst_ref=collected.at[me],
            send_sem=rs_send.at[tile], recv_sem=rs_recv,
            device_id=owner(tile), device_id_type=MESH,
        )

    def mine(tile):
        return (s == owner(tile)[0]) & (t == owner(tile)[1])

    for tile in range(TILES):
        @pl.when(jnp.logical_not(mine(tile)))
        def _():
            to_owner(tile).start()

    half = s % 2
    sibling = (s + 1 - 2 * half, t)

    def part(size):
        return pl.ds(pl.multiple_of(half * (size // 2), size // 2), size // 2)

    emb_part, gene_part = part(128), part(cols)
    across, along = [], []
    for d in range(1, tgt_n):
        peer = (s, (t + d) % tgt_n)
        other = (t + tgt_n - d) % tgt_n
        for a, (ref, held, piece) in enumerate(
            ((et_ref, emb, emb_part), (xt_ref, expr, emb_part), (genes.at[t], genes, gene_part))
        ):
            across.append(
                pltpu.make_async_remote_copy(
                    src_ref=ref.at[piece], dst_ref=held.at[t, piece],
                    send_sem=tgt_send.at[a, d - 1], recv_sem=tgt_recv.at[a, d - 1],
                    device_id=peer, device_id_type=MESH,
                )
            )
            along.append(
                pltpu.make_async_remote_copy(
                    src_ref=held.at[other, piece], dst_ref=held.at[other, piece],
                    send_sem=fw_send.at[a, d - 1], recv_sem=fw_recv.at[a, d - 1],
                    device_id=sibling, device_id_type=MESH,
                )
            )
    masses = [
        pltpu.make_async_remote_copy(
            src_ref=mt_ref, dst_ref=tmass.at[t],
            send_sem=tgt_send.at[3, d - 1], recv_sem=tgt_recv.at[3, d - 1],
            device_id=(s, (t + d) % tgt_n), device_id_type=MESH,
        )
        for d in range(1, tgt_n)
    ]
    fetch_genes.wait()
    for copy in across[0::3] + across[1::3] + masses + across[2::3]:
        copy.start()

    own_tile, owns = 0, False
    for tile in range(TILES):
        own_tile = jnp.where(mine(tile), tile, own_tile)
        owns = owns | mine(tile)

    @pl.when(owns)
    def _():
        collected[me] = partial[own_tile]
        whole = collected.at[pl.ds(0, n - 1)]
        pltpu.make_async_remote_copy(
            src_ref=whole, dst_ref=whole, send_sem=ag_send, recv_sem=rs_recv,
            device_id=place((me + 1) % n), device_id_type=MESH,
        ).wait_recv()
        core[own_tile] = jnp.sum(collected[...], axis=0)

        def spread(h, carry):
            pltpu.make_async_remote_copy(
                src_ref=core.at[own_tile], dst_ref=core.at[own_tile],
                send_sem=ag_send, recv_sem=ag_recv.at[own_tile],
                device_id=place((me + distant(h)) % n), device_id_type=MESH,
            ).start()
            return carry

        lax.fori_loop(0, n - 1, spread, 0)

    own = pl.ds(pl.multiple_of(base, 128), rows)
    fetch_expr.wait()
    q_high, q_mid, q_low = [right[129 + k:130 + k, own].astype(F32) for k in range(3)]
    f_pieces = [p.astype(F32) for p in split3(0.5 * fs_ref[:, own])]
    m_pieces = [p.astype(F32) for p in split3(ms_ref[:, own])]
    border[...] = jnp.zeros_like(border)
    border[0:16, :] = rows_of(
        16, rows, [q_high, q_high, q_high, q_mid, q_mid, q_low, 1.0, 1.0, 1.0] + f_pieces + m_pieces
    ).astype(BF16)
    pick = lax.broadcasted_iota(jnp.int32, (128, 128), 0)
    select = jnp.where((pick >= 12) & (pick < 15), 1.0, 0.0).astype(BF16)

    def turn_over(c, carry):
        at = pl.ds(pl.multiple_of(c * 128, 128), 128)
        e_rows = right[0:128, pl.ds(pl.multiple_of(base + c * 128, 128), 128)].T
        ends_rows = border[:, at].T
        lhs[at, 0:128] = xs[:, at].T
        lhs[at, 128:256] = e_rows
        lhs[at, 256:384] = e_rows
        lhs[at, 384:512] = ends_rows
        mass[at, :] = dot(ends_rows, select)
        return carry

    lax.fori_loop(0, rows // 128, turn_over, 0)

    for copy, onward in list(zip(across, along))[0::3] + list(zip(across, along))[1::3]:
        copy.wait_recv()
        onward.start()
    rhs[384:512, :] = jnp.zeros((128, nt), BF16)
    for copy in along[0::3] + along[1::3] + masses:
        copy.wait_recv()
    q_all = []
    for block in range(tgt_n):
        rhs[0:128, block * cols:(block + 1) * cols] = expr[block]
        e_wide = emb[block].astype(F32)
        q_all.append(jnp.sum(e_wide * e_wide, axis=0, keepdims=True))

    for tile in range(TILES):
        @pl.when(jnp.logical_not(mine(tile)))
        def _():
            pltpu.make_async_remote_copy(
                src_ref=core.at[tile], dst_ref=core.at[tile],
                send_sem=ag_send, recv_sem=ag_recv.at[tile],
                device_id=place((me + 1) % n), device_id_type=MESH,
            ).wait_recv()

    edge = core[16] * (1.0 / total_pairs)
    edge_cols = edge.T
    pieces = split3(core[...].reshape(TILES * 8, 128) * (1.0 / total_pairs))
    for block in range(tgt_n):
        at = slice(block * cols, (block + 1) * cols)
        e_t, q_t = emb[block], q_all[block]
        by_core = dot(pieces[0], e_t) + (dot(pieces[1], e_t) + dot(pieces[2], e_t))
        g_e = -2.0 * by_core[0:128, :] + edge_cols[:, 0:1] * q_t + edge_cols[:, 1:2]
        high, mid, unused = split3((-2.0 * GEOMETRY_WEIGHT) * g_e)
        rhs[128:256, at] = high
        rhs[256:384, at] = mid
        g_0 = -2.0 * by_core[130:131, :] + edge[4:5, 0:1] * q_t + edge[5:6, 0:1]
        g_1 = -2.0 * by_core[131:132, :] + edge[6:7, 0:1] * q_t + edge[7:8, 0:1]
        a_high, a_mid, a_low = [p.astype(F32) for p in split3(GEOMETRY_WEIGHT * g_0)]
        one_pieces = [p.astype(F32) for p in split3(GEOMETRY_WEIGHT * g_1)]
        rhs[384:400, at] = rows_of(
            16, cols, [a_high, a_mid, a_low, a_high, a_mid, a_high] + one_pieces + [1.0, 1.0, 1.0]
        ).astype(BF16)

    def share(turn, value):
        for c in range(lanes):
            slots[turn, me, c:c + 1, :] = value[:, c * 128:(c + 1) * 128]

        def send(h, carry):
            pltpu.make_async_remote_copy(
                src_ref=slots.at[turn, me], dst_ref=slots.at[turn, me],
                send_sem=col_send.at[turn], recv_sem=col_recv.at[turn],
                device_id=place((me + distant(h)) % n), device_id_type=MESH,
            ).start()
            return carry

        lax.fori_loop(0, n - 1, send, 0)
        whole = slots.at[turn, pl.ds(0, n - 1)]
        every = pltpu.make_async_remote_copy(
            src_ref=whole, dst_ref=whole, send_sem=col_send.at[turn], recv_sem=col_recv.at[turn],
            device_id=place((me + 1) % n), device_id_type=MESH,
        )
        every.wait_recv()
        return every

    colmax[...] = jnp.full_like(colmax, -1e30)
    colsum[...] = jnp.zeros_like(colsum)

    def scores(c, carry):
        at = pl.ds(pl.multiple_of(c * score_step, score_step), score_step)
        tile = dot(lhs[at, :], rhs[...]) * KAPPA
        score[at, :] = tile
        groups = tile.reshape(score_step // 8, 8, nt)
        before = colmax[...]
        now = jnp.maximum(before, jnp.max(groups, axis=0))
        colsum[...] = colsum[...] * jnp.exp2(before - now) + jnp.sum(jnp.exp2(groups - now[None]), axis=0)
        colmax[...] = now
        return carry

    lax.fori_loop(0, rows // score_step, scores, 0, unroll=2)
    tops = colmax[...]
    top = jnp.max(tops, axis=0, keepdims=True)
    first = share(0, top + jnp.log2(jnp.sum(colsum[...] * jnp.exp2(tops - top), axis=0, keepdims=True)))

    held = slots[0]
    top = jnp.max(held, axis=0)
    total = top + jnp.log2(jnp.sum(jnp.exp2(held - top[None]), axis=0))
    value = jnp.log2(tmass[...].reshape(lanes, 128)) - total
    for c in range(lanes):
        gpot[0:1, c * 128:(c + 1) * 128] = value[c:c + 1, :]
    for copy, onward in list(zip(across, along))[2::3]:
        copy.wait_recv()
        onward.start()
    colsum[...] = jnp.zeros_like(colsum)

    def middle_pass(c, carry):
        at = pl.ds(pl.multiple_of(c * middle_step, middle_step), middle_step)
        a = score[at, :] + gpot[...]
        p = jnp.exp2(a - jnp.max(a, axis=1, keepdims=True))
        share_of = mass[at, 0:1] / jnp.sum(p, axis=1, keepdims=True)
        colsum[...] += jnp.sum((p * share_of).reshape(middle_step // 8, 8, nt), axis=0)
        prob[at, :] = p.astype(BF16)
        return carry

    lax.fori_loop(0, rows // middle_step, middle_pass, 0, unroll=2)
    for copy in along[2::3]:
        copy.wait_recv()
    second = share(1, jnp.sum(colsum[...], axis=0, keepdims=True))

    scaling = (tmass[...].reshape(lanes, 128) / jnp.sum(slots[1], axis=0)).T
    for c in range(lanes):
        at = slice(c * 128, (c + 1) * 128)
        block, within = c * 128 // cols, c * 128 % cols
        column = scaling[:, c:c + 1]
        weighted[at, 0:gene_count] = (genes[block, within:within + 128, :].astype(F32) * column).astype(BF16)
        weighted[at, gene_count:gene_count + 128] = jnp.broadcast_to(column, (128, 128)).astype(BF16)

    def last_pass(c, carry):
        at = pl.ds(pl.multiple_of(c * last_step, last_step), last_step)
        both = dot(prob[at, :], weighted[...])
        inverse = 1.0 / both[:, gene_count:gene_count + 128]
        for k in range(gene_count // 128):
            lane = slice(k * 128, (k + 1) * 128)
            out_ref[at, lane] = (both[:, lane] * inverse).astype(BF16)
        return carry

    lax.fori_loop(0, rows // last_step, last_pass, 0, unroll=2)

    for copy in across + along + masses + [first, second]:
        copy.wait_send()
    for tile in range(TILES):
        @pl.when(jnp.logical_not(mine(tile)))
        def _():
            to_owner(tile).wait_send()

    @pl.when(owns)
    def _():
        whole = collected.at[pl.ds(0, n - 1)]
        pltpu.make_async_remote_copy(
            src_ref=whole, dst_ref=whole, send_sem=ag_send, recv_sem=rs_recv,
            device_id=place((me + 1) % n), device_id_type=MESH,
        ).wait_send()


def shards(src_n, tgt_n, es, et, xs, xt, plan, ms, mt, fs, genes):
    n = src_n * tgt_n
    local = es.shape[1]
    cols = et.shape[1]
    nt = cols * tgt_n
    rows = local // tgt_n
    total_pairs = float(local * src_n * nt)
    gene_count = genes.shape[1]
    score_step = min(rows, 256) if nt <= 1024 else 128
    middle_step = min(rows, 128) if nt <= 1024 else 64
    last_step = min(rows, 256)
    body = functools.partial(
        kernel, src_n, tgt_n, total_pairs, rows, score_step, middle_step, last_step
    )
    anywhere = pl.BlockSpec(memory_space=pl.ANY)
    vmem = pl.BlockSpec(memory_space=pltpu.VMEM)
    dma = pltpu.SemaphoreType.DMA
    return pl.pallas_call(
        body,
        out_shape=jax.ShapeDtypeStruct((rows, gene_count), BF16),
        in_specs=[anywhere, vmem, anywhere, vmem, anywhere, vmem, vmem, vmem, anywhere],
        out_specs=vmem,
        scratch_shapes=[
            pltpu.VMEM((144, local), BF16),
            pltpu.VMEM((local, cols), BF16),
            pltpu.VMEM((128, rows), BF16),
            pltpu.VMEM((tgt_n, 128, cols), BF16),
            pltpu.VMEM((tgt_n, 128, cols), BF16),
            pltpu.VMEM((tgt_n, cols // 128, 128), F32),
            pltpu.VMEM((tgt_n, cols, gene_count), BF16),
            pltpu.VMEM((TILES, 8, 128), F32),
            pltpu.VMEM((n, 8, 128), F32),
            pltpu.VMEM((TILES, 8, 128), F32),
            pltpu.VMEM((128, rows), BF16),
            pltpu.VMEM((rows, 512), BF16),
            pltpu.VMEM((rows, 128), F32),
            pltpu.VMEM((512, nt), BF16),
            pltpu.VMEM((rows, nt), F32),
            pltpu.VMEM((rows, nt), BF16),
            pltpu.VMEM((nt, gene_count + 128), BF16),
            pltpu.VMEM((2, n, nt // 128, 128), F32),
            pltpu.VMEM((1, nt), F32),
            pltpu.VMEM((8, nt), F32),
            pltpu.VMEM((8, nt), F32),
            dma((3 + CHUNKS,)),
            dma((4, tgt_n - 1)),
            dma((4, tgt_n - 1)),
            dma((3, tgt_n - 1)),
            dma((3, tgt_n - 1)),
            dma((TILES,)),
            dma,
            dma,
            dma((TILES,)),
            dma((2,)),
            dma((2,)),
        ],
        compiler_params=pltpu.CompilerParams(
            collective_id=0, has_side_effects=True, vmem_limit_bytes=56 * 1024 * 1024
        ),
    )(
        es, et, xs, xt, plan,
        ms.reshape(1, local), mt.reshape(cols // 128, 128), fs.reshape(1, local), genes,
    )


def solution(mesh):
    src_n = mesh.shape["src"]
    tgt_n = mesh.shape["tgt"]
    return jax.shard_map(
        functools.partial(shards, src_n, tgt_n),
        mesh=mesh,
        in_specs=(
            P(None, "src"),
            P(None, "tgt"),
            P(None, "src"),
            P(None, "tgt"),
            P("src", "tgt"),
            P("src"),
            P("tgt"),
            P("src"),
            P("tgt", None),
        ),
        out_specs=P(("src", "tgt"), None),
        check_vma=False,
    )
```

```python
import functools
import math

import jax
import jax.numpy as jnp
from jax import lax
from jax.experimental import pallas as pl
from jax.experimental.pallas import tpu as pltpu
from jax.sharding import PartitionSpec as P

EPSILON = 0.05
GEOMETRY_WEIGHT = 4.0
LOG2E = math.log2(math.e)
KAPPA = 2.0 * LOG2E / EPSILON
MESH = pl.DeviceIdType.MESH
F32 = jnp.float32
BF16 = jnp.bfloat16
TILES = 17
CHUNKS = 4


def split3(value):
    high = value.astype(BF16)
    rest = value - high.astype(F32)
    middle = rest.astype(BF16)
    low = (rest - middle.astype(F32)).astype(BF16)
    return high, middle, low


def dot(a, b, dims=((1,), (0,))):
    return lax.dot_general(a, b, (dims, ((), ())), preferred_element_type=F32)


def dot3(a, b, dims=((1,), (0,))):
    high, middle, low = split3(a)
    return dot(high, b, dims) + (dot(middle, b, dims) + dot(low, b, dims))


def rows_of(count, width, values):
    row = lax.broadcasted_iota(jnp.int32, (count, width), 0)
    held = jnp.zeros((count, width), F32)
    for k, value in enumerate(values):
        held = jnp.where(row == k, value, held)
    return held


def kernel(
    src_n, tgt_n, total_pairs, rows, score_step, middle_step,
    es_ref, et_ref, xs_ref, xt_ref, plan_ref, ms_ref, mt_ref, fs_ref, genes_ref,
    prob, weighted, scale_row,
    right, plan, xs, masses_row, potentials, emb, expr, tmass, genes, partial, collected, core,
    border, lhs, mass, rhs, score, slots, gpot, colmax, colsum,
    in_sem, tgt_send, tgt_recv, fw_send, fw_recv, rs_send, rs_recv, ag_send, ag_recv,
    col_send, col_recv,
):
    n = src_n * tgt_n
    s = lax.axis_index("src")
    t = lax.axis_index("tgt")
    me = s * tgt_n + t
    cols = et_ref.shape[1]
    nt = cols * tgt_n
    local = es_ref.shape[1]
    lanes = nt // 128
    gene_count = genes_ref.shape[1]
    base = t * rows
    own = pl.ds(pl.multiple_of(base, 128), rows)

    def place(linear):
        return (linear // tgt_n, linear % tgt_n)

    def distant(h):
        return n // 2 + (1 - 2 * (h % 2)) * ((h + 1) // 2)

    def owner(tile):
        if tile < 16:
            return (src_n // 2 - 4 + tile // 2, (tile % 2) * (tgt_n // 2))
        return (src_n // 2 + 4, 0)

    barrier = pltpu.get_barrier_semaphore()

    def greet(h, carry):
        pl.semaphore_signal(
            barrier, inc=1, device_id=place((me + distant(h)) % n), device_id_type=MESH
        )
        return carry

    lax.fori_loop(0, n - 1, greet, 0)

    plan_step = local // CHUNKS
    fetch_embed = pltpu.make_async_copy(es_ref, right.at[0:128], in_sem.at[0])
    fetch_plan = [
        pltpu.make_async_copy(
            plan_ref.at[c * plan_step:(c + 1) * plan_step],
            plan.at[c * plan_step:(c + 1) * plan_step], in_sem.at[3 + c],
        )
        for c in range(CHUNKS)
    ]
    fetch_expr = pltpu.make_async_copy(
        xs_ref.at[:, pl.ds(pl.multiple_of(base, 128), rows)], xs, in_sem.at[1]
    )
    fetch_genes = pltpu.make_async_copy(genes_ref, genes.at[t], in_sem.at[2])
    at_target = (pltpu.make_async_copy(et_ref, emb.at[t], in_sem.at[3 + CHUNKS]),
                 pltpu.make_async_copy(xt_ref, expr.at[t], in_sem.at[4 + CHUNKS]),
                 pltpu.make_async_copy(mt_ref, tmass.at[t], in_sem.at[5 + CHUNKS]))
    at_source = (pltpu.make_async_copy(ms_ref.at[:, own], masses_row, in_sem.at[6 + CHUNKS]),
                 pltpu.make_async_copy(fs_ref.at[:, own], potentials, in_sem.at[7 + CHUNKS]))
    for copy in (at_target[0], fetch_embed) + tuple(fetch_plan) + at_target[1:] + at_source + (fetch_expr, fetch_genes):
        copy.start()
    at_target[0].wait()
    target = emb[t]
    target_wide = target.astype(F32)
    q_tgt = [p.astype(F32) for p in split3(jnp.sum(target_wide * target_wide, axis=0, keepdims=True))]
    fetch_embed.wait()

    wide = right[0:128, :].astype(F32)
    q_src = [p.astype(F32) for p in split3(jnp.sum(wide * wide, axis=0, keepdims=True))]
    right[128:144, :] = rows_of(16, local, [1.0] + q_src).astype(BF16)

    here = 0.0
    for c in range(CHUNKS):
        fetch_plan[c].wait()
        at = slice(c * plan_step, (c + 1) * plan_step)
        here = here + dot(right[:, at], plan[at, :])
    by_e = here[0:128, :]
    by_one = here[128:129, :]
    by_q = here[129:130, :] + (here[130:131, :] + here[131:132, :])
    high, mid, low = split3(by_e)
    across_dims = ((1,), (1,))
    partial[0:16] = (
        dot(high, target, across_dims) + (dot(mid, target, across_dims) + dot(low, target, across_dims))
    ).reshape(16, 8, 128)
    ends = rows_of(16, cols, [1.0] + q_tgt).astype(BF16)
    ends = dot(ends, high, across_dims) + (dot(ends, mid, across_dims) + dot(ends, low, across_dims))
    q_wide = q_tgt[0] + (q_tgt[1] + q_tgt[2])
    row = lax.broadcasted_iota(jnp.int32, (8, 128), 0)
    edge_t = jnp.where(row == 0, ends[0:1, :], jnp.where(row == 1, ends[1:2, :] + (ends[2:3, :] + ends[3:4, :]), 0.0))
    sums = rows_of(8, cols, [0.0, 0.0, by_one, by_q])
    scalars = rows_of(8, cols, [0.0, 0.0, 0.0, 0.0, by_one, by_one * q_wide, by_q, by_q * q_wide])
    partial[16] = edge_t + dot3(sums, target, across_dims) + jnp.sum(scalars, axis=1, keepdims=True)

    pl.semaphore_wait(barrier, n - 1)

    def to_owner(tile):
        return pltpu.make_async_remote_copy(
            src_ref=partial.at[tile], dst_ref=collected.at[me],
            send_sem=rs_send.at[tile], recv_sem=rs_recv,
            device_id=owner(tile), device_id_type=MESH,
        )

    def mine(tile):
        return (s == owner(tile)[0]) & (t == owner(tile)[1])

    for tile in range(TILES):
        @pl.when(jnp.logical_not(mine(tile)))
        def _():
            to_owner(tile).start()

    half = s % 2
    sibling = (s + 1 - 2 * half, t)

    def part(size):
        return pl.ds(pl.multiple_of(half * (size // 2), size // 2), size // 2)

    emb_part, gene_part = part(128), part(cols)
    across, along = [], []
    for d in range(1, tgt_n):
        peer = (s, (t + d) % tgt_n)
        other = (t + tgt_n - d) % tgt_n
        for a, (ref, held, piece) in enumerate(
            ((emb.at[t], emb, emb_part), (expr.at[t], expr, emb_part), (genes.at[t], genes, gene_part))
        ):
            across.append(
                pltpu.make_async_remote_copy(
                    src_ref=ref.at[piece], dst_ref=held.at[t, piece],
                    send_sem=tgt_send.at[a, d - 1], recv_sem=tgt_recv.at[a, d - 1],
                    device_id=peer, device_id_type=MESH,
                )
            )
            along.append(
                pltpu.make_async_remote_copy(
                    src_ref=held.at[other, piece], dst_ref=held.at[other, piece],
                    send_sem=fw_send.at[a, d - 1], recv_sem=fw_recv.at[a, d - 1],
                    device_id=sibling, device_id_type=MESH,
                )
            )
    masses = [
        pltpu.make_async_remote_copy(
            src_ref=tmass.at[t], dst_ref=tmass.at[t],
            send_sem=tgt_send.at[3, d - 1], recv_sem=tgt_recv.at[3, d - 1],
            device_id=(s, (t + d) % tgt_n), device_id_type=MESH,
        )
        for d in range(1, tgt_n)
    ]
    for copy in at_target[1:] + (fetch_genes,):
        copy.wait()
    for copy in across[0::3] + across[1::3] + masses + across[2::3]:
        copy.start()

    own_tile, owns = 0, False
    for tile in range(TILES):
        own_tile = jnp.where(mine(tile), tile, own_tile)
        owns = owns | mine(tile)

    @pl.when(owns)
    def _():
        collected[me] = partial[own_tile]
        whole = collected.at[pl.ds(0, n - 1)]
        pltpu.make_async_remote_copy(
            src_ref=whole, dst_ref=whole, send_sem=ag_send, recv_sem=rs_recv,
            device_id=place((me + 1) % n), device_id_type=MESH,
        ).wait_recv()
        core[own_tile] = jnp.sum(collected[...], axis=0)

        def spread(h, carry):
            pltpu.make_async_remote_copy(
                src_ref=core.at[own_tile], dst_ref=core.at[own_tile],
                send_sem=ag_send, recv_sem=ag_recv.at[own_tile],
                device_id=place((me + distant(h)) % n), device_id_type=MESH,
            ).start()
            return carry

        lax.fori_loop(0, n - 1, spread, 0)

    fetch_expr.wait()
    for copy in at_source:
        copy.wait()
    q_high, q_mid, q_low = [right[129 + k:130 + k, own].astype(F32) for k in range(3)]
    f_pieces = [p.astype(F32) for p in split3(0.5 * potentials[...])]
    m_pieces = [p.astype(F32) for p in split3(masses_row[...])]
    border[...] = jnp.zeros_like(border)
    border[0:16, :] = rows_of(
        16, rows, [q_high, q_high, q_high, q_mid, q_mid, q_low, 1.0, 1.0, 1.0] + f_pieces + m_pieces
    ).astype(BF16)
    pick = lax.broadcasted_iota(jnp.int32, (128, 128), 0)
    select = jnp.where((pick >= 12) & (pick < 15), 1.0, 0.0).astype(BF16)

    def turn_over(c, carry):
        at = pl.ds(pl.multiple_of(c * 128, 128), 128)
        e_rows = right[0:128, pl.ds(pl.multiple_of(base + c * 128, 128), 128)].T
        ends_rows = border[:, at].T
        lhs[at, 0:128] = xs[:, at].T
        lhs[at, 128:256] = e_rows
        lhs[at, 256:384] = e_rows
        lhs[at, 384:512] = ends_rows
        mass[at, :] = dot(ends_rows, select)
        return carry

    lax.fori_loop(0, rows // 128, turn_over, 0)

    for copy, onward in list(zip(across, along))[0::3] + list(zip(across, along))[1::3]:
        copy.wait_recv()
        onward.start()
    rhs[384:512, :] = jnp.zeros((128, nt), BF16)
    for copy in along[0::3] + along[1::3] + masses:
        copy.wait_recv()
    q_all = []
    for block in range(tgt_n):
        rhs[0:128, block * cols:(block + 1) * cols] = expr[block]
        e_wide = emb[block].astype(F32)
        q_all.append(jnp.sum(e_wide * e_wide, axis=0, keepdims=True))

    for tile in range(TILES):
        @pl.when(jnp.logical_not(mine(tile)))
        def _():
            pltpu.make_async_remote_copy(
                src_ref=core.at[tile], dst_ref=core.at[tile],
                send_sem=ag_send, recv_sem=ag_recv.at[tile],
                device_id=place((me + 1) % n), device_id_type=MESH,
            ).wait_recv()

    edge = core[16] * (1.0 / total_pairs)
    edge_cols = edge.T
    pieces = split3(core[...].reshape(TILES * 8, 128) * (1.0 / total_pairs))
    for block in range(tgt_n):
        at = slice(block * cols, (block + 1) * cols)
        e_t, q_t = emb[block], q_all[block]
        by_core = dot(pieces[0], e_t) + (dot(pieces[1], e_t) + dot(pieces[2], e_t))
        g_e = -2.0 * by_core[0:128, :] + edge_cols[:, 0:1] * q_t + edge_cols[:, 1:2]
        high, mid, unused = split3((-2.0 * GEOMETRY_WEIGHT) * g_e)
        rhs[128:256, at] = high
        rhs[256:384, at] = mid
        g_0 = -2.0 * by_core[130:131, :] + edge[4:5, 0:1] * q_t + edge[5:6, 0:1]
        g_1 = -2.0 * by_core[131:132, :] + edge[6:7, 0:1] * q_t + edge[7:8, 0:1]
        a_high, a_mid, a_low = [p.astype(F32) for p in split3(GEOMETRY_WEIGHT * g_0)]
        one_pieces = [p.astype(F32) for p in split3(GEOMETRY_WEIGHT * g_1)]
        rhs[384:400, at] = rows_of(
            16, cols, [a_high, a_mid, a_low, a_high, a_mid, a_high] + one_pieces + [1.0, 1.0, 1.0]
        ).astype(BF16)

    def share(turn, value):
        for c in range(lanes):
            slots[turn, me, c:c + 1, :] = value[:, c * 128:(c + 1) * 128]

        def send(h, carry):
            pltpu.make_async_remote_copy(
                src_ref=slots.at[turn, me], dst_ref=slots.at[turn, me],
                send_sem=col_send.at[turn], recv_sem=col_recv.at[turn],
                device_id=place((me + distant(h)) % n), device_id_type=MESH,
            ).start()
            return carry

        lax.fori_loop(0, n - 1, send, 0)
        whole = slots.at[turn, pl.ds(0, n - 1)]
        every = pltpu.make_async_remote_copy(
            src_ref=whole, dst_ref=whole, send_sem=col_send.at[turn], recv_sem=col_recv.at[turn],
            device_id=place((me + 1) % n), device_id_type=MESH,
        )
        every.wait_recv()
        return every

    colmax[...] = jnp.full_like(colmax, -1e30)
    colsum[...] = jnp.zeros_like(colsum)

    def scores(c, carry):
        at = pl.ds(pl.multiple_of(c * score_step, score_step), score_step)
        tile = dot(lhs[at, :], rhs[...]) * KAPPA
        score[at, :] = tile
        groups = tile.reshape(score_step // 8, 8, nt)
        before = colmax[...]
        now = jnp.maximum(before, jnp.max(groups, axis=0))
        colsum[...] = colsum[...] * jnp.exp2(before - now) + jnp.sum(jnp.exp2(groups - now[None]), axis=0)
        colmax[...] = now
        return carry

    lax.fori_loop(0, rows // score_step, scores, 0, unroll=2)
    tops = colmax[...]
    top = jnp.max(tops, axis=0, keepdims=True)
    first = share(0, top + jnp.log2(jnp.sum(colsum[...] * jnp.exp2(tops - top), axis=0, keepdims=True)))

    held = slots[0]
    top = jnp.max(held, axis=0)
    total = top + jnp.log2(jnp.sum(jnp.exp2(held - top[None]), axis=0))
    value = jnp.log2(tmass[...].reshape(lanes, 128)) - total
    for c in range(lanes):
        gpot[0:1, c * 128:(c + 1) * 128] = value[c:c + 1, :]
    for copy, onward in list(zip(across, along))[2::3]:
        copy.wait_recv()
        onward.start()
    colsum[...] = jnp.zeros_like(colsum)

    def middle_pass(c, carry):
        at = pl.ds(pl.multiple_of(c * middle_step, middle_step), middle_step)
        a = score[at, :] + gpot[...]
        p = jnp.exp2(a - jnp.max(a, axis=1, keepdims=True))
        share_of = mass[at, 0:1] / jnp.sum(p, axis=1, keepdims=True)
        colsum[...] += jnp.sum((p * share_of).reshape(middle_step // 8, 8, nt), axis=0)
        prob[at, :] = p.astype(BF16)
        return carry

    lax.fori_loop(0, rows // middle_step, middle_pass, 0, unroll=2)
    for copy in along[2::3]:
        copy.wait_recv()
    second = share(1, jnp.sum(colsum[...], axis=0, keepdims=True))

    scaling = tmass[...].reshape(lanes, 128) / jnp.sum(slots[1], axis=0)
    columns = scaling.T
    for c in range(lanes):
        at = slice(c * 128, (c + 1) * 128)
        block, within = c * 128 // cols, c * 128 % cols
        scale_row[:, at] = jnp.broadcast_to(scaling[c:c + 1, :], (8, 128))
        weighted[at, :] = (genes[block, within:within + 128, :].astype(F32) * columns[:, c:c + 1]).astype(BF16)

    for copy in across + along + masses + [first, second]:
        copy.wait_send()
    for tile in range(TILES):
        @pl.when(jnp.logical_not(mine(tile)))
        def _():
            to_owner(tile).wait_send()

    @pl.when(owns)
    def _():
        whole = collected.at[pl.ds(0, n - 1)]
        pltpu.make_async_remote_copy(
            src_ref=whole, dst_ref=whole, send_sem=ag_send, recv_sem=rs_recv,
            device_id=place((me + 1) % n), device_id_type=MESH,
        ).wait_send()


def finish(prob_ref, weighted_ref, scale_ref, out_ref, held, sems, *, last_step):
    rows = prob_ref.shape[0]
    copies = []
    for c in range(rows // last_step):
        at = slice(c * last_step, (c + 1) * last_step)
        p = prob_ref[at, :]
        total = jnp.sum(p.astype(F32) * scale_ref[0:1, :], axis=1, keepdims=True)
        held[at, :] = (dot(p, weighted_ref[...]) * (1.0 / total)).astype(BF16)
        copy = pltpu.make_async_copy(held.at[at], out_ref.at[at], sems.at[c])
        copy.start()
        copies.append(copy)
    for copy in copies:
        copy.wait()


def shards(src_n, tgt_n, es, et, xs, xt, plan, ms, mt, fs, genes):
    n = src_n * tgt_n
    local = es.shape[1]
    cols = et.shape[1]
    nt = cols * tgt_n
    rows = local // tgt_n
    total_pairs = float(local * src_n * nt)
    gene_count = genes.shape[1]
    score_step = min(rows, 256) if nt <= 1024 else 128
    middle_step = min(rows, 256) if nt <= 1024 else 64
    last_step = min(rows, 256)
    body = functools.partial(
        kernel, src_n, tgt_n, total_pairs, rows, score_step, middle_step
    )
    hbm = pl.BlockSpec(memory_space=pltpu.HBM)
    vmem = pl.BlockSpec(memory_space=pltpu.VMEM)
    dma = pltpu.SemaphoreType.DMA
    prob, weighted, scale_row = pl.pallas_call(
        body,
        out_shape=[pltpu.VMEM((rows, nt), BF16), pltpu.VMEM((nt, gene_count), BF16), pltpu.VMEM((8, nt), F32)],
        in_specs=[hbm] * 9,
        out_specs=[vmem, vmem, vmem],
        scratch_shapes=[
            pltpu.VMEM((144, local), BF16),
            pltpu.VMEM((local, cols), BF16),
            pltpu.VMEM((128, rows), BF16),
            pltpu.VMEM((1, rows), F32),
            pltpu.VMEM((1, rows), F32),
            pltpu.VMEM((tgt_n, 128, cols), BF16),
            pltpu.VMEM((tgt_n, 128, cols), BF16),
            pltpu.VMEM((tgt_n, cols // 128, 128), F32),
            pltpu.VMEM((tgt_n, cols, gene_count), BF16),
            pltpu.VMEM((TILES, 8, 128), F32),
            pltpu.VMEM((n, 8, 128), F32),
            pltpu.VMEM((TILES, 8, 128), F32),
            pltpu.VMEM((128, rows), BF16),
            pltpu.VMEM((rows, 512), BF16),
            pltpu.VMEM((rows, 128), F32),
            pltpu.VMEM((512, nt), BF16),
            pltpu.VMEM((rows, nt), F32),
            pltpu.VMEM((2, n, nt // 128, 128), F32),
            pltpu.VMEM((1, nt), F32),
            pltpu.VMEM((8, nt), F32),
            pltpu.VMEM((8, nt), F32),
            dma((8 + CHUNKS,)),
            dma((4, tgt_n - 1)),
            dma((4, tgt_n - 1)),
            dma((3, tgt_n - 1)),
            dma((3, tgt_n - 1)),
            dma((TILES,)),
            dma,
            dma,
            dma((TILES,)),
            dma((2,)),
            dma((2,)),
        ],
        compiler_params=pltpu.CompilerParams(
            collective_id=0, has_side_effects=True, vmem_limit_bytes=40 * 1024 * 1024
        ),
    )(*[
        pltpu.with_memory_space_constraint(value, pltpu.HBM)
        for value in (
            es, et, xs, xt, plan,
            ms.reshape(1, local), mt.reshape(cols // 128, 128), fs.reshape(1, local), genes,
        )
    ])
    return pl.pallas_call(
        functools.partial(finish, last_step=last_step),
        out_shape=jax.ShapeDtypeStruct((rows, gene_count), BF16),
        in_specs=[vmem, vmem, vmem],
        out_specs=hbm,
        scratch_shapes=[pltpu.VMEM((rows, gene_count), BF16), dma((rows // last_step,))],
        compiler_params=pltpu.CompilerParams(vmem_limit_bytes=16 * 1024 * 1024),
    )(
        pltpu.with_memory_space_constraint(prob, pltpu.VMEM),
        pltpu.with_memory_space_constraint(weighted, pltpu.VMEM),
        pltpu.with_memory_space_constraint(scale_row, pltpu.VMEM),
    )


def solution(mesh):
    src_n = mesh.shape["src"]
    tgt_n = mesh.shape["tgt"]
    return jax.shard_map(
        functools.partial(shards, src_n, tgt_n),
        mesh=mesh,
        in_specs=(
            P(None, "src"),
            P(None, "tgt"),
            P(None, "src"),
            P(None, "tgt"),
            P("src", "tgt"),
            P("src"),
            P("tgt"),
            P("src"),
            P("tgt", None),
        ),
        out_specs=P(("src", "tgt"), None),
        check_vma=False,
    )
```

```python
import functools
import math

import jax
import jax.numpy as jnp
from jax import lax
from jax.experimental import pallas as pl
from jax.experimental.pallas import tpu as pltpu
from jax.sharding import PartitionSpec as P

EPSILON = 0.05
GEOMETRY_WEIGHT = 4.0
LOG2E = math.log2(math.e)
KAPPA = 2.0 * LOG2E / EPSILON
MESH = pl.DeviceIdType.MESH
F32 = jnp.float32
BF16 = jnp.bfloat16
TILES = 17
CHUNKS = 4


def split3(value):
    high = value.astype(BF16)
    rest = value - high.astype(F32)
    middle = rest.astype(BF16)
    low = (rest - middle.astype(F32)).astype(BF16)
    return high, middle, low


def dot(a, b, dims=((1,), (0,))):
    return lax.dot_general(a, b, (dims, ((), ())), preferred_element_type=F32)


def dot3(a, b, dims=((1,), (0,))):
    high, middle, low = split3(a)
    return dot(high, b, dims) + (dot(middle, b, dims) + dot(low, b, dims))


def rows_of(count, width, values):
    row = lax.broadcasted_iota(jnp.int32, (count, width), 0)
    held = jnp.zeros((count, width), F32)
    for k, value in enumerate(values):
        held = jnp.where(row == k, value, held)
    return held


def kernel(
    src_n, tgt_n, total_pairs, rows, score_step, middle_step,
    es_ref, et_ref, xs_ref, xt_ref, plan_ref, ms_ref, mt_ref, fs_ref, genes_ref,
    prob, weighted, scale_row,
    right, plan, xs, masses_row, potentials, emb, expr, tmass, genes, partial, collected, core,
    border, lhs, mass, rhs, score, slots, gpot, colsum,
    in_sem, tgt_send, tgt_recv, fw_send, fw_recv, rs_send, rs_recv, ag_send, ag_recv,
    col_send, col_recv,
):
    n = src_n * tgt_n
    s = lax.axis_index("src")
    t = lax.axis_index("tgt")
    me = s * tgt_n + t
    cols = et_ref.shape[1]
    nt = cols * tgt_n
    local = es_ref.shape[1]
    lanes = nt // 128
    gene_count = genes_ref.shape[1]
    base = t * rows
    own = pl.ds(pl.multiple_of(base, 128), rows)

    def place(linear):
        return (linear // tgt_n, linear % tgt_n)

    planes = src_n // 4
    hops = sorted(
        (
            -min(dz, planes - dz) - dx - dy,
            (dz, dx, dc, dy),
        )
        for dz in range(planes) for dx in range(2) for dc in range(2) for dy in range(tgt_n)
        if dz + dx + dc + dy
    )

    def everyone(act):
        if n > 64:
            def one(k, carry):
                act(place((me + n // 2 + k) % n))
                return carry

            lax.fori_loop(0, n // 2, one, 0)
            lax.fori_loop(n // 2 + 1, n, one, 0)
            return
        for unused, (dz, dx, dc, dy) in hops:
            plane = s // 4 if dz == 0 else (s // 4 + dz) % planes
            column = s // 2 % 2 if dx == 0 else 1 - s // 2 % 2
            core_of = s % 2 if dc == 0 else 1 - s % 2
            act((plane * 4 + column * 2 + core_of, t if dy == 0 else (t + dy) % tgt_n))

    def owner(tile):
        if tile < 16:
            return (src_n // 2 - 4 + tile // 2, (tile % 2) * (tgt_n // 2))
        return (src_n // 2 + 4, 0)

    barrier = pltpu.get_barrier_semaphore()

    def greet(device):
        pl.semaphore_signal(
            barrier, inc=1, device_id=device, device_id_type=MESH
        )

    everyone(greet)

    plan_step = local // CHUNKS
    fetch_embed = pltpu.make_async_copy(es_ref, right.at[0:128], in_sem.at[0])
    fetch_plan = [
        pltpu.make_async_copy(
            plan_ref.at[c * plan_step:(c + 1) * plan_step],
            plan.at[c * plan_step:(c + 1) * plan_step], in_sem.at[3 + c],
        )
        for c in range(CHUNKS)
    ]
    fetch_expr = pltpu.make_async_copy(
        xs_ref.at[:, pl.ds(pl.multiple_of(base, 128), rows)], xs, in_sem.at[1]
    )
    fetch_genes = pltpu.make_async_copy(genes_ref, genes.at[t], in_sem.at[2])
    at_target = (pltpu.make_async_copy(et_ref, emb.at[t], in_sem.at[3 + CHUNKS]),
                 pltpu.make_async_copy(xt_ref, expr.at[t], in_sem.at[4 + CHUNKS]),
                 pltpu.make_async_copy(mt_ref, tmass.at[t], in_sem.at[5 + CHUNKS]))
    at_source = (pltpu.make_async_copy(ms_ref.at[:, own], masses_row, in_sem.at[6 + CHUNKS]),
                 pltpu.make_async_copy(fs_ref.at[:, own], potentials, in_sem.at[7 + CHUNKS]))
    for copy in (at_target[0], fetch_embed) + tuple(fetch_plan):
        copy.start()
    at_target[0].wait()
    target = emb[t]
    target_wide = target.astype(F32)
    q_tgt = [p.astype(F32) for p in split3(jnp.sum(target_wide * target_wide, axis=0, keepdims=True))]
    fetch_embed.wait()

    wide = right[0:128, :].astype(F32)
    q_src = [p.astype(F32) for p in split3(jnp.sum(wide * wide, axis=0, keepdims=True))]
    right[128:144, :] = rows_of(16, local, [1.0] + q_src).astype(BF16)

    here = 0.0
    for c in range(CHUNKS):
        fetch_plan[c].wait()
        at = slice(c * plan_step, (c + 1) * plan_step)
        here = here + dot(right[:, at], plan[at, :])
    for copy in at_target[1:] + at_source + (fetch_expr, fetch_genes):
        copy.start()
    by_e = here[0:128, :]
    by_one = here[128:129, :]
    by_q = here[129:130, :] + (here[130:131, :] + here[131:132, :])
    high, mid, low = split3(by_e)
    across_dims = ((1,), (1,))
    partial[0:16] = (
        dot(high, target, across_dims) + (dot(mid, target, across_dims) + dot(low, target, across_dims))
    ).reshape(16, 8, 128)
    ends = rows_of(16, cols, [1.0] + q_tgt).astype(BF16)
    ends = dot(ends, high, across_dims) + (dot(ends, mid, across_dims) + dot(ends, low, across_dims))
    q_wide = q_tgt[0] + (q_tgt[1] + q_tgt[2])
    row = lax.broadcasted_iota(jnp.int32, (8, 128), 0)
    edge_t = jnp.where(row == 0, ends[0:1, :], jnp.where(row == 1, ends[1:2, :] + (ends[2:3, :] + ends[3:4, :]), 0.0))
    sums = rows_of(8, cols, [0.0, 0.0, by_one, by_q])
    scalars = rows_of(8, cols, [0.0, 0.0, 0.0, 0.0, by_one, by_one * q_wide, by_q, by_q * q_wide])
    partial[16] = edge_t + dot3(sums, target, across_dims) + jnp.sum(scalars, axis=1, keepdims=True)

    pl.semaphore_wait(barrier, n - 1)

    def to_owner(tile):
        return pltpu.make_async_remote_copy(
            src_ref=partial.at[tile], dst_ref=collected.at[me],
            send_sem=rs_send.at[tile], recv_sem=rs_recv,
            device_id=owner(tile), device_id_type=MESH,
        )

    def mine(tile):
        return (s == owner(tile)[0]) & (t == owner(tile)[1])

    for tile in range(TILES):
        @pl.when(jnp.logical_not(mine(tile)))
        def _():
            to_owner(tile).start()

    half = s % 2
    sibling = (s + 1 - 2 * half, t)

    def part(size):
        return pl.ds(pl.multiple_of(half * (size // 2), size // 2), size // 2)

    emb_part, gene_part = part(128), part(cols)
    across, along = [], []
    for d in range(1, tgt_n):
        peer = (s, (t + d) % tgt_n)
        other = (t + tgt_n - d) % tgt_n
        for a, (ref, held, piece) in enumerate(
            ((emb.at[t], emb, emb_part), (expr.at[t], expr, emb_part), (genes.at[t], genes, gene_part))
        ):
            across.append(
                pltpu.make_async_remote_copy(
                    src_ref=ref.at[piece], dst_ref=held.at[t, piece],
                    send_sem=tgt_send.at[a, d - 1], recv_sem=tgt_recv.at[a, d - 1],
                    device_id=peer, device_id_type=MESH,
                )
            )
            along.append(
                pltpu.make_async_remote_copy(
                    src_ref=held.at[other, piece], dst_ref=held.at[other, piece],
                    send_sem=fw_send.at[a, d - 1], recv_sem=fw_recv.at[a, d - 1],
                    device_id=sibling, device_id_type=MESH,
                )
            )
    masses = [
        pltpu.make_async_remote_copy(
            src_ref=tmass.at[t], dst_ref=tmass.at[t],
            send_sem=tgt_send.at[3, d - 1], recv_sem=tgt_recv.at[3, d - 1],
            device_id=(s, (t + d) % tgt_n), device_id_type=MESH,
        )
        for d in range(1, tgt_n)
    ]
    for copy in at_target[1:] + (fetch_genes,):
        copy.wait()
    for copy in across[0::3] + across[1::3] + masses + across[2::3]:
        copy.start()

    own_tile, owns = 0, False
    for tile in range(TILES):
        own_tile = jnp.where(mine(tile), tile, own_tile)
        owns = owns | mine(tile)

    @pl.when(owns)
    def _():
        collected[me] = partial[own_tile]
        whole = collected.at[pl.ds(0, n - 1)]
        pltpu.make_async_remote_copy(
            src_ref=whole, dst_ref=whole, send_sem=ag_send, recv_sem=rs_recv,
            device_id=place((me + 1) % n), device_id_type=MESH,
        ).wait_recv()
        core[own_tile] = jnp.sum(collected[...], axis=0)

        def spread(device):
            pltpu.make_async_remote_copy(
                src_ref=core.at[own_tile], dst_ref=core.at[own_tile],
                send_sem=ag_send, recv_sem=ag_recv.at[own_tile],
                device_id=device, device_id_type=MESH,
            ).start()

        everyone(spread)

    fetch_expr.wait()
    for copy in at_source:
        copy.wait()
    q_high, q_mid, q_low = [right[129 + k:130 + k, own].astype(F32) for k in range(3)]
    f_pieces = [p.astype(F32) for p in split3(0.5 * potentials[...])]
    m_pieces = [p.astype(F32) for p in split3(masses_row[...])]
    border[...] = jnp.zeros_like(border)
    border[0:16, :] = rows_of(
        16, rows, [q_high, q_high, q_high, q_mid, q_mid, q_low, 1.0, 1.0, 1.0] + f_pieces + m_pieces
    ).astype(BF16)
    pick = lax.broadcasted_iota(jnp.int32, (128, 128), 0)
    select = jnp.where((pick >= 12) & (pick < 15), 1.0, 0.0).astype(BF16)

    def turn_over(c, carry):
        at = pl.ds(pl.multiple_of(c * 128, 128), 128)
        e_rows = right[0:128, pl.ds(pl.multiple_of(base + c * 128, 128), 128)].T
        ends_rows = border[:, at].T
        lhs[at, 0:128] = xs[:, at].T
        lhs[at, 128:256] = e_rows
        lhs[at, 256:384] = e_rows
        lhs[at, 384:512] = ends_rows
        mass[at, :] = dot(ends_rows, select)
        return carry

    lax.fori_loop(0, rows // 128, turn_over, 0)

    for copy, onward in list(zip(across, along))[0::3] + list(zip(across, along))[1::3]:
        copy.wait_recv()
        onward.start()
    rhs[384:512, :] = jnp.zeros((128, nt), BF16)
    for copy in along[0::3] + along[1::3] + masses:
        copy.wait_recv()
    q_all = []
    for block in range(tgt_n):
        rhs[0:128, block * cols:(block + 1) * cols] = expr[block]
        e_wide = emb[block].astype(F32)
        q_all.append(jnp.sum(e_wide * e_wide, axis=0, keepdims=True))

    for tile in range(TILES):
        @pl.when(jnp.logical_not(mine(tile)))
        def _():
            pltpu.make_async_remote_copy(
                src_ref=core.at[tile], dst_ref=core.at[tile],
                send_sem=ag_send, recv_sem=ag_recv.at[tile],
                device_id=place((me + 1) % n), device_id_type=MESH,
            ).wait_recv()

    edge = core[16] * (1.0 / total_pairs)
    edge_cols = edge.T
    pieces = split3(core[...].reshape(TILES * 8, 128) * (1.0 / total_pairs))
    for block in range(tgt_n):
        at = slice(block * cols, (block + 1) * cols)
        e_t, q_t = emb[block], q_all[block]
        by_core = dot(pieces[0], e_t) + (dot(pieces[1], e_t) + dot(pieces[2], e_t))
        g_e = -2.0 * by_core[0:128, :] + edge_cols[:, 0:1] * q_t + edge_cols[:, 1:2]
        high, mid, unused = split3((-2.0 * GEOMETRY_WEIGHT) * g_e)
        rhs[128:256, at] = high
        rhs[256:384, at] = mid
        g_0 = -2.0 * by_core[130:131, :] + edge[4:5, 0:1] * q_t + edge[5:6, 0:1]
        g_1 = -2.0 * by_core[131:132, :] + edge[6:7, 0:1] * q_t + edge[7:8, 0:1]
        a_high, a_mid, a_low = [p.astype(F32) for p in split3(GEOMETRY_WEIGHT * g_0)]
        one_pieces = [p.astype(F32) for p in split3(GEOMETRY_WEIGHT * g_1)]
        rhs[384:400, at] = rows_of(
            16, cols, [a_high, a_mid, a_low, a_high, a_mid, a_high] + one_pieces + [1.0, 1.0, 1.0]
        ).astype(BF16)

    def share(turn, value):
        for c in range(lanes):
            slots[turn, me, c:c + 1, :] = value[:, c * 128:(c + 1) * 128]

        def send(device):
            pltpu.make_async_remote_copy(
                src_ref=slots.at[turn, me], dst_ref=slots.at[turn, me],
                send_sem=col_send.at[turn], recv_sem=col_recv.at[turn],
                device_id=device, device_id_type=MESH,
            ).start()

        everyone(send)
        whole = slots.at[turn, pl.ds(0, n - 1)]
        every = pltpu.make_async_remote_copy(
            src_ref=whole, dst_ref=whole, send_sem=col_send.at[turn], recv_sem=col_recv.at[turn],
            device_id=place((me + 1) % n), device_id_type=MESH,
        )
        every.wait_recv()
        return every

    def scores(r, k):
        at, lane = slice(r * score_step, (r + 1) * score_step), slice(k * 256, (k + 1) * 256)
        tile = dot(lhs[at, :], rhs[:, lane]) * KAPPA
        score[at, lane] = tile
        return jnp.max(tile.reshape(score_step // 8, 8, 256), axis=0)

    def fold(r, k, top):
        at, lane = slice(r * score_step, (r + 1) * score_step), slice(k * 256, (k + 1) * 256)
        return jnp.sum(jnp.exp2(score[at, lane].reshape(score_step // 8, 8, 256) - top[None]), axis=0)

    def ended(k, top, total):
        whole = jnp.max(top, axis=0, keepdims=True)
        total = jnp.sum(total * jnp.exp2(top - whole), axis=0, keepdims=True)
        return whole + jnp.log2(total)

    blocks, tiles = rows // score_step, nt // 256
    done, last = [], None
    for k in range(tiles):
        top, total = -1e30, 0.0
        for r in range(blocks):
            top = jnp.maximum(top, scores(r, k))
            if k:
                total = total + fold(r, k - 1, last)
        if k:
            done.append(ended(k - 1, last, total))
        last = top
    total = 0.0
    for r in range(blocks):
        total = total + fold(r, tiles - 1, last)
    done.append(ended(tiles - 1, last, total))
    first = share(0, jnp.concatenate(done, axis=1))

    held = slots[0]
    top = jnp.max(held, axis=0)
    total = top + jnp.log2(jnp.sum(jnp.exp2(held - top[None]), axis=0))
    value = jnp.log2(tmass[...].reshape(lanes, 128)) - total
    for c in range(lanes):
        gpot[0:1, c * 128:(c + 1) * 128] = value[c:c + 1, :]
    for copy, onward in list(zip(across, along))[2::3]:
        copy.wait_recv()
        onward.start()
    colsum[...] = jnp.zeros_like(colsum)

    def middle_pass(c, carry):
        at = pl.ds(pl.multiple_of(c * middle_step, middle_step), middle_step)
        a = score[at, :] + gpot[...]
        p = jnp.exp2(a - jnp.max(a, axis=1, keepdims=True))
        share_of = mass[at, 0:1] / jnp.sum(p, axis=1, keepdims=True)
        colsum[...] += jnp.sum((p * share_of).reshape(middle_step // 8, 8, nt), axis=0)
        prob[at, :] = p.astype(BF16)
        return carry

    lax.fori_loop(0, rows // middle_step, middle_pass, 0, unroll=2)
    for copy in along[2::3]:
        copy.wait_recv()
    second = share(1, jnp.sum(colsum[...], axis=0, keepdims=True))

    scaling = tmass[...].reshape(lanes, 128) / jnp.sum(slots[1], axis=0)
    columns = scaling.T
    for c in range(lanes):
        at = slice(c * 128, (c + 1) * 128)
        block, within = c * 128 // cols, c * 128 % cols
        scale_row[:, at] = jnp.broadcast_to(scaling[c:c + 1, :], (8, 128))
        weighted[at, :] = (genes[block, within:within + 128, :].astype(F32) * columns[:, c:c + 1]).astype(BF16)

    for copy in across + along + masses + [first, second]:
        copy.wait_send()
    for tile in range(TILES):
        @pl.when(jnp.logical_not(mine(tile)))
        def _():
            to_owner(tile).wait_send()

    @pl.when(owns)
    def _():
        whole = collected.at[pl.ds(0, n - 1)]
        pltpu.make_async_remote_copy(
            src_ref=whole, dst_ref=whole, send_sem=ag_send, recv_sem=rs_recv,
            device_id=place((me + 1) % n), device_id_type=MESH,
        ).wait_send()


def finish(prob_ref, weighted_ref, scale_ref, out_ref, held, sems, *, last_step):
    rows = prob_ref.shape[0]
    copies = []
    for c in range(rows // last_step):
        at = slice(c * last_step, (c + 1) * last_step)
        p = prob_ref[at, :]
        total = jnp.sum(p.astype(F32) * scale_ref[0:1, :], axis=1, keepdims=True)
        held[at, :] = (dot(p, weighted_ref[...]) * (1.0 / total)).astype(BF16)
        copy = pltpu.make_async_copy(held.at[at], out_ref.at[at], sems.at[c])
        copy.start()
        copies.append(copy)
    for copy in copies:
        copy.wait()


def shards(src_n, tgt_n, es, et, xs, xt, plan, ms, mt, fs, genes):
    n = src_n * tgt_n
    local = es.shape[1]
    cols = et.shape[1]
    nt = cols * tgt_n
    rows = local // tgt_n
    total_pairs = float(local * src_n * nt)
    gene_count = genes.shape[1]
    score_step = min(rows, 512) if nt <= 1024 else 128
    middle_step = min(rows, 256) if nt <= 1024 else 64
    last_step = min(rows, 256)
    body = functools.partial(
        kernel, src_n, tgt_n, total_pairs, rows, score_step, middle_step
    )
    hbm = pl.BlockSpec(memory_space=pltpu.HBM)
    vmem = pl.BlockSpec(memory_space=pltpu.VMEM)
    dma = pltpu.SemaphoreType.DMA
    prob, weighted, scale_row = pl.pallas_call(
        body,
        out_shape=[pltpu.VMEM((rows, nt), BF16), pltpu.VMEM((nt, gene_count), BF16), pltpu.VMEM((8, nt), F32)],
        in_specs=[hbm] * 9,
        out_specs=[vmem, vmem, vmem],
        scratch_shapes=[
            pltpu.VMEM((144, local), BF16),
            pltpu.VMEM((local, cols), BF16),
            pltpu.VMEM((128, rows), BF16),
            pltpu.VMEM((1, rows), F32),
            pltpu.VMEM((1, rows), F32),
            pltpu.VMEM((tgt_n, 128, cols), BF16),
            pltpu.VMEM((tgt_n, 128, cols), BF16),
            pltpu.VMEM((tgt_n, cols // 128, 128), F32),
            pltpu.VMEM((tgt_n, cols, gene_count), BF16),
            pltpu.VMEM((TILES, 8, 128), F32),
            pltpu.VMEM((n, 8, 128), F32),
            pltpu.VMEM((TILES, 8, 128), F32),
            pltpu.VMEM((128, rows), BF16),
            pltpu.VMEM((rows, 512), BF16),
            pltpu.VMEM((rows, 128), F32),
            pltpu.VMEM((512, nt), BF16),
            pltpu.VMEM((rows, nt), F32),
            pltpu.VMEM((2, n, nt // 128, 128), F32),
            pltpu.VMEM((1, nt), F32),
            pltpu.VMEM((8, nt), F32),
            dma((8 + CHUNKS,)),
            dma((4, tgt_n - 1)),
            dma((4, tgt_n - 1)),
            dma((3, tgt_n - 1)),
            dma((3, tgt_n - 1)),
            dma((TILES,)),
            dma,
            dma,
            dma((TILES,)),
            dma((2,)),
            dma((2,)),
        ],
        compiler_params=pltpu.CompilerParams(
            collective_id=0, has_side_effects=True, vmem_limit_bytes=40 * 1024 * 1024
        ),
    )(*[
        pltpu.with_memory_space_constraint(value, pltpu.HBM)
        for value in (
            es, et, xs, xt, plan,
            ms.reshape(1, local), mt.reshape(cols // 128, 128), fs.reshape(1, local), genes,
        )
    ])
    return pl.pallas_call(
        functools.partial(finish, last_step=last_step),
        out_shape=jax.ShapeDtypeStruct((rows, gene_count), BF16),
        in_specs=[vmem, vmem, vmem],
        out_specs=hbm,
        scratch_shapes=[pltpu.VMEM((rows, gene_count), BF16), dma((rows // last_step,))],
        compiler_params=pltpu.CompilerParams(vmem_limit_bytes=16 * 1024 * 1024),
    )(
        pltpu.with_memory_space_constraint(prob, pltpu.VMEM),
        pltpu.with_memory_space_constraint(weighted, pltpu.VMEM),
        pltpu.with_memory_space_constraint(scale_row, pltpu.VMEM),
    )


def solution(mesh):
    src_n = mesh.shape["src"]
    tgt_n = mesh.shape["tgt"]
    return jax.shard_map(
        functools.partial(shards, src_n, tgt_n),
        mesh=mesh,
        in_specs=(
            P(None, "src"),
            P(None, "tgt"),
            P(None, "src"),
            P(None, "tgt"),
            P("src", "tgt"),
            P("src"),
            P("tgt"),
            P("src"),
            P("tgt", None),
        ),
        out_specs=P(("src", "tgt"), None),
        check_vma=False,
    )
```

```python
import functools
import math

import jax
import jax.numpy as jnp
from jax import lax
from jax.experimental import pallas as pl
from jax.experimental.pallas import tpu as pltpu
from jax.sharding import PartitionSpec as P

EPSILON = 0.05
GEOMETRY_WEIGHT = 4.0
LOG2E = math.log2(math.e)
KAPPA = 2.0 * LOG2E / EPSILON
MESH = pl.DeviceIdType.MESH
F32 = jnp.float32
BF16 = jnp.bfloat16
TILES = 17
CHUNKS = 4
PARTS = 2


def split3(value):
    high = value.astype(BF16)
    rest = value - high.astype(F32)
    middle = rest.astype(BF16)
    low = (rest - middle.astype(F32)).astype(BF16)
    return high, middle, low


def dot(a, b, dims=((1,), (0,))):
    return lax.dot_general(a, b, (dims, ((), ())), preferred_element_type=F32)


def dot3(a, b, dims=((1,), (0,))):
    high, middle, low = split3(a)
    return dot(high, b, dims) + (dot(middle, b, dims) + dot(low, b, dims))


def rows_of(count, width, values):
    row = lax.broadcasted_iota(jnp.int32, (count, width), 0)
    held = jnp.zeros((count, width), F32)
    for k, value in enumerate(values):
        held = jnp.where(row == k, value, held)
    return held


def kernel(
    src_n, tgt_n, total_pairs, rows, score_step, middle_step,
    es_ref, et_ref, xs_ref, xt_ref, plan_ref, ms_ref, mt_ref, fs_ref, genes_ref,
    prob, weighted, scale_row,
    right, plan, xs, masses_row, potentials, emb, expr, tmass, genes, partial, collected, core,
    border, lhs, mass, rhs, score, logs, totals, staged, gpot, colsum,
    in_sem, tgt_send, tgt_recv, fw_send, fw_recv, rs_send, rs_recv, ag_send, ag_recv,
    col_send, col_recv,
):
    n = src_n * tgt_n
    s = lax.axis_index("src")
    t = lax.axis_index("tgt")
    me = s * tgt_n + t
    cols = et_ref.shape[1]
    nt = cols * tgt_n
    local = es_ref.shape[1]
    lanes = nt // 128
    gene_count = genes_ref.shape[1]
    base = t * rows
    own = pl.ds(pl.multiple_of(base, 128), rows)

    def place(linear):
        return (linear // tgt_n, linear % tgt_n)

    planes = src_n // 4
    hops = sorted(
        (
            -min(dz, planes - dz) - dx - dy,
            (dz, dx, dc, dy),
        )
        for dz in range(planes) for dx in range(2) for dc in range(2) for dy in range(tgt_n)
        if dz + dx + dc + dy
    )

    def everyone(act):
        if n > 64:
            def one(k, carry):
                act(place((me + n // 2 + k) % n))
                return carry

            lax.fori_loop(0, n // 2, one, 0)
            lax.fori_loop(n // 2 + 1, n, one, 0)
            return
        for unused, (dz, dx, dc, dy) in hops:
            plane = s // 4 if dz == 0 else (s // 4 + dz) % planes
            column = s // 2 % 2 if dx == 0 else 1 - s // 2 % 2
            core_of = s % 2 if dc == 0 else 1 - s % 2
            act((plane * 4 + column * 2 + core_of, t if dy == 0 else (t + dy) % tgt_n))

    def owner(tile):
        if tile < 16:
            return (src_n // 2 - 4 + tile // 2, (tile % 2) * (tgt_n // 2))
        return (src_n // 2 + 4, 0)

    barrier = pltpu.get_barrier_semaphore()

    def greet(device):
        pl.semaphore_signal(
            barrier, inc=1, device_id=device, device_id_type=MESH
        )

    everyone(greet)

    plan_step = local // CHUNKS
    fetch_embed = pltpu.make_async_copy(es_ref, right.at[0:128], in_sem.at[0])
    fetch_plan = [
        pltpu.make_async_copy(
            plan_ref.at[c * plan_step:(c + 1) * plan_step],
            plan.at[c * plan_step:(c + 1) * plan_step], in_sem.at[3 + c],
        )
        for c in range(CHUNKS)
    ]
    fetch_expr = pltpu.make_async_copy(
        xs_ref.at[:, pl.ds(pl.multiple_of(base, 128), rows)], xs, in_sem.at[1]
    )
    fetch_genes = pltpu.make_async_copy(genes_ref, genes.at[t], in_sem.at[2])
    at_target = (pltpu.make_async_copy(et_ref, emb.at[t], in_sem.at[3 + CHUNKS]),
                 pltpu.make_async_copy(xt_ref, expr.at[t], in_sem.at[4 + CHUNKS]),
                 pltpu.make_async_copy(mt_ref, tmass.at[t], in_sem.at[5 + CHUNKS]))
    at_source = (pltpu.make_async_copy(ms_ref.at[:, own], masses_row, in_sem.at[6 + CHUNKS]),
                 pltpu.make_async_copy(fs_ref.at[:, own], potentials, in_sem.at[7 + CHUNKS]))
    for copy in (at_target[0], fetch_embed) + tuple(fetch_plan):
        copy.start()
    at_target[0].wait()
    target = emb[t]
    target_wide = target.astype(F32)
    q_tgt = [p.astype(F32) for p in split3(jnp.sum(target_wide * target_wide, axis=0, keepdims=True))]
    fetch_embed.wait()

    wide = right[0:128, :].astype(F32)
    q_src = [p.astype(F32) for p in split3(jnp.sum(wide * wide, axis=0, keepdims=True))]
    right[128:144, :] = rows_of(16, local, [1.0] + q_src).astype(BF16)

    here = 0.0
    for c in range(CHUNKS):
        fetch_plan[c].wait()
        at = slice(c * plan_step, (c + 1) * plan_step)
        here = here + dot(right[:, at], plan[at, :])
    for copy in at_target[1:] + at_source + (fetch_expr, fetch_genes):
        copy.start()
    by_e = here[0:128, :]
    by_one = here[128:129, :]
    by_q = here[129:130, :] + (here[130:131, :] + here[131:132, :])
    high, mid, low = split3(by_e)
    across_dims = ((1,), (1,))
    partial[0:16] = (
        dot(high, target, across_dims) + (dot(mid, target, across_dims) + dot(low, target, across_dims))
    ).reshape(16, 8, 128)
    ends = rows_of(16, cols, [1.0] + q_tgt).astype(BF16)
    ends = dot(ends, high, across_dims) + (dot(ends, mid, across_dims) + dot(ends, low, across_dims))
    q_wide = q_tgt[0] + (q_tgt[1] + q_tgt[2])
    row = lax.broadcasted_iota(jnp.int32, (8, 128), 0)
    edge_t = jnp.where(row == 0, ends[0:1, :], jnp.where(row == 1, ends[1:2, :] + (ends[2:3, :] + ends[3:4, :]), 0.0))
    sums = rows_of(8, cols, [0.0, 0.0, by_one, by_q])
    scalars = rows_of(8, cols, [0.0, 0.0, 0.0, 0.0, by_one, by_one * q_wide, by_q, by_q * q_wide])
    partial[16] = edge_t + dot3(sums, target, across_dims) + jnp.sum(scalars, axis=1, keepdims=True)

    pl.semaphore_wait(barrier, n - 1)

    def to_owner(tile):
        return pltpu.make_async_remote_copy(
            src_ref=partial.at[tile], dst_ref=collected.at[me],
            send_sem=rs_send.at[tile], recv_sem=rs_recv,
            device_id=owner(tile), device_id_type=MESH,
        )

    def mine(tile):
        return (s == owner(tile)[0]) & (t == owner(tile)[1])

    for tile in range(TILES):
        @pl.when(jnp.logical_not(mine(tile)))
        def _():
            to_owner(tile).start()

    half = s % 2
    sibling = (s + 1 - 2 * half, t)

    def part(size):
        return pl.ds(pl.multiple_of(half * (size // 2), size // 2), size // 2)

    emb_part, gene_part = part(128), part(cols)
    across, along = [], []
    for d in range(1, tgt_n):
        peer = (s, (t + d) % tgt_n)
        other = (t + tgt_n - d) % tgt_n
        for a, (ref, held, piece) in enumerate(
            ((emb.at[t], emb, emb_part), (expr.at[t], expr, emb_part), (genes.at[t], genes, gene_part))
        ):
            across.append(
                pltpu.make_async_remote_copy(
                    src_ref=ref.at[piece], dst_ref=held.at[t, piece],
                    send_sem=tgt_send.at[a, d - 1], recv_sem=tgt_recv.at[a, d - 1],
                    device_id=peer, device_id_type=MESH,
                )
            )
            along.append(
                pltpu.make_async_remote_copy(
                    src_ref=held.at[other, piece], dst_ref=held.at[other, piece],
                    send_sem=fw_send.at[a, d - 1], recv_sem=fw_recv.at[a, d - 1],
                    device_id=sibling, device_id_type=MESH,
                )
            )
    masses = [
        pltpu.make_async_remote_copy(
            src_ref=tmass.at[t], dst_ref=tmass.at[t],
            send_sem=tgt_send.at[3, d - 1], recv_sem=tgt_recv.at[3, d - 1],
            device_id=(s, (t + d) % tgt_n), device_id_type=MESH,
        )
        for d in range(1, tgt_n)
    ]
    for copy in at_target[1:] + (fetch_genes,):
        copy.wait()
    for copy in across[0::3] + across[1::3] + masses + across[2::3]:
        copy.start()

    own_tile, owns = 0, False
    for tile in range(TILES):
        own_tile = jnp.where(mine(tile), tile, own_tile)
        owns = owns | mine(tile)

    @pl.when(owns)
    def _():
        collected[me] = partial[own_tile]
        whole = collected.at[pl.ds(0, n - 1)]
        pltpu.make_async_remote_copy(
            src_ref=whole, dst_ref=whole, send_sem=ag_send, recv_sem=rs_recv,
            device_id=place((me + 1) % n), device_id_type=MESH,
        ).wait_recv()
        core[own_tile] = jnp.sum(collected[...], axis=0)

        def spread(device):
            pltpu.make_async_remote_copy(
                src_ref=core.at[own_tile], dst_ref=core.at[own_tile],
                send_sem=ag_send, recv_sem=ag_recv.at[own_tile],
                device_id=device, device_id_type=MESH,
            ).start()

        everyone(spread)

    fetch_expr.wait()
    for copy in at_source:
        copy.wait()
    q_high, q_mid, q_low = [right[129 + k:130 + k, own].astype(F32) for k in range(3)]
    f_pieces = [p.astype(F32) for p in split3(0.5 * potentials[...])]
    m_pieces = [p.astype(F32) for p in split3(masses_row[...])]
    border[...] = jnp.zeros_like(border)
    border[0:16, :] = rows_of(
        16, rows, [q_high, q_high, q_high, q_mid, q_mid, q_low, 1.0, 1.0, 1.0] + f_pieces + m_pieces
    ).astype(BF16)
    pick = lax.broadcasted_iota(jnp.int32, (128, 128), 0)
    select = jnp.where((pick >= 12) & (pick < 15), 1.0, 0.0).astype(BF16)

    def turn_over(c, carry):
        at = pl.ds(pl.multiple_of(c * 128, 128), 128)
        e_rows = right[0:128, pl.ds(pl.multiple_of(base + c * 128, 128), 128)].T
        ends_rows = border[:, at].T
        lhs[at, 0:128] = xs[:, at].T
        lhs[at, 128:256] = e_rows
        lhs[at, 256:384] = e_rows
        lhs[at, 384:512] = ends_rows
        mass[at, :] = dot(ends_rows, select)
        return carry

    lax.fori_loop(0, rows // 128, turn_over, 0)

    for copy, onward in list(zip(across, along))[0::3] + list(zip(across, along))[1::3]:
        copy.wait_recv()
        onward.start()
    rhs[384:512, :] = jnp.zeros((128, nt), BF16)
    for copy in along[0::3] + along[1::3] + masses:
        copy.wait_recv()
    q_all = []
    for block in range(tgt_n):
        rhs[0:128, block * cols:(block + 1) * cols] = expr[block]
        e_wide = emb[block].astype(F32)
        q_all.append(jnp.sum(e_wide * e_wide, axis=0, keepdims=True))

    for tile in range(TILES):
        @pl.when(jnp.logical_not(mine(tile)))
        def _():
            pltpu.make_async_remote_copy(
                src_ref=core.at[tile], dst_ref=core.at[tile],
                send_sem=ag_send, recv_sem=ag_recv.at[tile],
                device_id=place((me + 1) % n), device_id_type=MESH,
            ).wait_recv()

    edge = core[16] * (1.0 / total_pairs)
    edge_cols = edge.T
    pieces = split3(core[...].reshape(TILES * 8, 128) * (1.0 / total_pairs))
    for block in range(tgt_n):
        at = slice(block * cols, (block + 1) * cols)
        e_t, q_t = emb[block], q_all[block]
        by_core = dot(pieces[0], e_t) + (dot(pieces[1], e_t) + dot(pieces[2], e_t))
        g_e = -2.0 * by_core[0:128, :] + edge_cols[:, 0:1] * q_t + edge_cols[:, 1:2]
        high, mid, unused = split3((-2.0 * GEOMETRY_WEIGHT) * g_e)
        rhs[128:256, at] = high
        rhs[256:384, at] = mid
        g_0 = -2.0 * by_core[130:131, :] + edge[4:5, 0:1] * q_t + edge[5:6, 0:1]
        g_1 = -2.0 * by_core[131:132, :] + edge[6:7, 0:1] * q_t + edge[7:8, 0:1]
        a_high, a_mid, a_low = [p.astype(F32) for p in split3(GEOMETRY_WEIGHT * g_0)]
        one_pieces = [p.astype(F32) for p in split3(GEOMETRY_WEIGHT * g_1)]
        rhs[384:400, at] = rows_of(
            16, cols, [a_high, a_mid, a_low, a_high, a_mid, a_high] + one_pieces + [1.0, 1.0, 1.0]
        ).astype(BF16)

    def share(turn, value):
        slots = logs.at[turn] if turn < PARTS else totals
        for c in range(value.shape[1] // 128):
            staged[c:c + 1, :] = value[:, c * 128:(c + 1) * 128]
        slots[me] = staged[0:value.shape[1] // 128, :].astype(slots.dtype)

        def send(device):
            pltpu.make_async_remote_copy(
                src_ref=slots.at[me], dst_ref=slots.at[me],
                send_sem=col_send.at[turn], recv_sem=col_recv.at[turn],
                device_id=device, device_id_type=MESH,
            ).start()

        everyone(send)
        whole = slots.at[pl.ds(0, n - 1)]
        every = pltpu.make_async_remote_copy(
            src_ref=whole, dst_ref=whole, send_sem=col_send.at[turn], recv_sem=col_recv.at[turn],
            device_id=place((me + 1) % n), device_id_type=MESH,
        )
        return every

    def scores(r, k):
        at, lane = slice(r * score_step, (r + 1) * score_step), slice(k * 256, (k + 1) * 256)
        tile = dot(lhs[at, :], rhs[:, lane]) * KAPPA
        score[at, lane] = tile
        return jnp.max(tile.reshape(score_step // 8, 8, 256), axis=0)

    def fold(r, k, top):
        at, lane = slice(r * score_step, (r + 1) * score_step), slice(k * 256, (k + 1) * 256)
        return jnp.sum(jnp.exp2(score[at, lane].reshape(score_step // 8, 8, 256) - top[None]), axis=0)

    def ended(k, top, total):
        whole = jnp.max(top, axis=0, keepdims=True)
        total = jnp.sum(total * jnp.exp2(top - whole), axis=0, keepdims=True)
        return whole + jnp.log2(total)

    blocks, tiles = rows // score_step, nt // 256
    done, last, first = [], None, []
    for k in range(tiles):
        top, total = -1e30, 0.0
        for r in range(blocks):
            top = jnp.maximum(top, scores(r, k))
            if k:
                total = total + fold(r, k - 1, last)
        if k:
            done.append(ended(k - 1, last, total))
            if k % (tiles // PARTS) == 0:
                first.append(share(k // (tiles // PARTS) - 1, jnp.concatenate(done[k - tiles // PARTS:], axis=1)))
        last = top
    total = 0.0
    for r in range(blocks):
        total = total + fold(r, tiles - 1, last)
    done.append(ended(tiles - 1, last, total))
    first.append(share(PARTS - 1, jnp.concatenate(done[len(done) - tiles // PARTS:], axis=1)))

    target_logs = jnp.log2(tmass[...].reshape(lanes, 128))
    some = lanes // PARTS
    for part_at, every in enumerate(first):
        every.wait_recv()
        held = logs[part_at]
        top = jnp.max(held, axis=0)
        total = top + jnp.log2(jnp.sum(jnp.exp2(held - top[None]), axis=0))
        value = target_logs[part_at * some:(part_at + 1) * some, :] - total
        for c in range(some):
            gpot[0:1, (part_at * some + c) * 128:(part_at * some + c + 1) * 128] = value[c:c + 1, :]
    for copy, onward in list(zip(across, along))[2::3]:
        copy.wait_recv()
        onward.start()
    colsum[...] = jnp.zeros_like(colsum)

    def middle_pass(c, carry):
        at = pl.ds(pl.multiple_of(c * middle_step, middle_step), middle_step)
        a = score[at, :] + gpot[...]
        p = jnp.exp2(a - jnp.max(a, axis=1, keepdims=True))
        share_of = mass[at, 0:1] / jnp.sum(p, axis=1, keepdims=True)
        colsum[...] += jnp.sum((p * share_of).reshape(middle_step // 8, 8, nt), axis=0)
        prob[at, :] = p.astype(BF16)
        return carry

    lax.fori_loop(0, rows // middle_step, middle_pass, 0, unroll=2)
    for copy in along[2::3]:
        copy.wait_recv()
    second = share(PARTS, jnp.sum(colsum[...], axis=0, keepdims=True))
    second.wait_recv()

    scaling = tmass[...].reshape(lanes, 128) / jnp.sum(totals[...].astype(F32), axis=0)
    columns = scaling.T
    for c in range(lanes):
        at = slice(c * 128, (c + 1) * 128)
        block, within = c * 128 // cols, c * 128 % cols
        scale_row[:, at] = jnp.broadcast_to(scaling[c:c + 1, :], (8, 128))
        weighted[at, :] = (genes[block, within:within + 128, :].astype(F32) * columns[:, c:c + 1]).astype(BF16)

    for copy in across + along + masses + first + [second]:
        copy.wait_send()
    for tile in range(TILES):
        @pl.when(jnp.logical_not(mine(tile)))
        def _():
            to_owner(tile).wait_send()

    @pl.when(owns)
    def _():
        whole = collected.at[pl.ds(0, n - 1)]
        pltpu.make_async_remote_copy(
            src_ref=whole, dst_ref=whole, send_sem=ag_send, recv_sem=rs_recv,
            device_id=place((me + 1) % n), device_id_type=MESH,
        ).wait_send()


def finish(prob_ref, weighted_ref, scale_ref, out_ref, held, sems, *, last_step):
    rows = prob_ref.shape[0]
    copies = []
    for c in range(rows // last_step):
        at = slice(c * last_step, (c + 1) * last_step)
        p = prob_ref[at, :]
        total = jnp.sum(p.astype(F32) * scale_ref[0:1, :], axis=1, keepdims=True)
        held[at, :] = (dot(p, weighted_ref[...]) * (1.0 / total)).astype(BF16)
        copy = pltpu.make_async_copy(held.at[at], out_ref.at[at], sems.at[c])
        copy.start()
        copies.append(copy)
    for copy in copies:
        copy.wait()


def shards(src_n, tgt_n, es, et, xs, xt, plan, ms, mt, fs, genes):
    n = src_n * tgt_n
    local = es.shape[1]
    cols = et.shape[1]
    nt = cols * tgt_n
    rows = local // tgt_n
    total_pairs = float(local * src_n * nt)
    gene_count = genes.shape[1]
    score_step = min(rows, 512) if nt <= 1024 else 128
    middle_step = min(rows, 256) if nt <= 1024 else 64
    last_step = min(rows, 256)
    body = functools.partial(
        kernel, src_n, tgt_n, total_pairs, rows, score_step, middle_step
    )
    hbm = pl.BlockSpec(memory_space=pltpu.HBM)
    vmem = pl.BlockSpec(memory_space=pltpu.VMEM)
    dma = pltpu.SemaphoreType.DMA
    prob, weighted, scale_row = pl.pallas_call(
        body,
        out_shape=[pltpu.VMEM((rows, nt), BF16), pltpu.VMEM((nt, gene_count), BF16), pltpu.VMEM((8, nt), F32)],
        in_specs=[hbm] * 9,
        out_specs=[vmem, vmem, vmem],
        scratch_shapes=[
            pltpu.VMEM((144, local), BF16),
            pltpu.VMEM((local, cols), BF16),
            pltpu.VMEM((128, rows), BF16),
            pltpu.VMEM((1, rows), F32),
            pltpu.VMEM((1, rows), F32),
            pltpu.VMEM((tgt_n, 128, cols), BF16),
            pltpu.VMEM((tgt_n, 128, cols), BF16),
            pltpu.VMEM((tgt_n, cols // 128, 128), F32),
            pltpu.VMEM((tgt_n, cols, gene_count), BF16),
            pltpu.VMEM((TILES, 8, 128), F32),
            pltpu.VMEM((n, 8, 128), F32),
            pltpu.VMEM((TILES, 8, 128), F32),
            pltpu.VMEM((128, rows), BF16),
            pltpu.VMEM((rows, 512), BF16),
            pltpu.VMEM((rows, 128), F32),
            pltpu.VMEM((512, nt), BF16),
            pltpu.VMEM((rows, nt), F32),
            pltpu.VMEM((PARTS, n, nt // 128 // PARTS, 128), F32),
            pltpu.VMEM((n, nt // 128, 128), BF16),
            pltpu.VMEM((nt // 128, 128), F32),
            pltpu.VMEM((1, nt), F32),
            pltpu.VMEM((8, nt), F32),
            dma((8 + CHUNKS,)),
            dma((4, tgt_n - 1)),
            dma((4, tgt_n - 1)),
            dma((3, tgt_n - 1)),
            dma((3, tgt_n - 1)),
            dma((TILES,)),
            dma,
            dma,
            dma((TILES,)),
            dma((PARTS + 1,)),
            dma((PARTS + 1,)),
        ],
        compiler_params=pltpu.CompilerParams(
            collective_id=0, has_side_effects=True, vmem_limit_bytes=40 * 1024 * 1024
        ),
    )(*[
        pltpu.with_memory_space_constraint(value, pltpu.HBM)
        for value in (
            es, et, xs, xt, plan,
            ms.reshape(1, local), mt.reshape(cols // 128, 128), fs.reshape(1, local), genes,
        )
    ])
    return pl.pallas_call(
        functools.partial(finish, last_step=last_step),
        out_shape=jax.ShapeDtypeStruct((rows, gene_count), BF16),
        in_specs=[vmem, vmem, vmem],
        out_specs=hbm,
        scratch_shapes=[pltpu.VMEM((rows, gene_count), BF16), dma((rows // last_step,))],
        compiler_params=pltpu.CompilerParams(vmem_limit_bytes=16 * 1024 * 1024),
    )(
        pltpu.with_memory_space_constraint(prob, pltpu.VMEM),
        pltpu.with_memory_space_constraint(weighted, pltpu.VMEM),
        pltpu.with_memory_space_constraint(scale_row, pltpu.VMEM),
    )


def solution(mesh):
    src_n = mesh.shape["src"]
    tgt_n = mesh.shape["tgt"]
    return jax.shard_map(
        functools.partial(shards, src_n, tgt_n),
        mesh=mesh,
        in_specs=(
            P(None, "src"),
            P(None, "tgt"),
            P(None, "src"),
            P(None, "tgt"),
            P("src", "tgt"),
            P("src"),
            P("tgt"),
            P("src"),
            P("tgt", None),
        ),
        out_specs=P(("src", "tgt"), None),
        check_vma=False,
    )
```

```python
import functools
import math

import jax
import jax.numpy as jnp
from jax import lax
from jax.experimental import pallas as pl
from jax.experimental.pallas import tpu as pltpu
from jax.sharding import PartitionSpec as P

EPSILON = 0.05
GEOMETRY_WEIGHT = 4.0
LOG2E = math.log2(math.e)
KAPPA = 2.0 * LOG2E / EPSILON
MESH = pl.DeviceIdType.MESH
F32 = jnp.float32
BF16 = jnp.bfloat16
TILES = 17
CHUNKS = 4
PARTS = 2


def split3(value):
    high = value.astype(BF16)
    rest = value - high.astype(F32)
    middle = rest.astype(BF16)
    low = (rest - middle.astype(F32)).astype(BF16)
    return high, middle, low


def dot(a, b, dims=((1,), (0,))):
    return lax.dot_general(a, b, (dims, ((), ())), preferred_element_type=F32)


def dot3(a, b, dims=((1,), (0,))):
    high, middle, low = split3(a)
    return dot(high, b, dims) + (dot(middle, b, dims) + dot(low, b, dims))


def rows_of(count, width, values):
    row = lax.broadcasted_iota(jnp.int32, (count, width), 0)
    held = jnp.zeros((count, width), F32)
    for k, value in enumerate(values):
        held = jnp.where(row == k, value, held)
    return held


def kernel(
    src_n, tgt_n, total_pairs, rows, score_step, middle_step,
    es_ref, et_ref, xs_ref, xt_ref, plan_ref, ms_ref, mt_ref, fs_ref, genes_ref,
    prob, weighted, scale_row, factors,
    right, plan, xs, masses_row, potentials, emb, expr, tmass, genes, partial, collected, core,
    border, lhs, mass, rhs, score, logs, totals, staged, gpot,
    in_sem, tgt_send, tgt_recv, fw_send, fw_recv, rs_send, rs_recv, ag_send, ag_recv,
    col_send, col_recv,
):
    n = src_n * tgt_n
    s = lax.axis_index("src")
    t = lax.axis_index("tgt")
    me = s * tgt_n + t
    cols = et_ref.shape[1]
    nt = cols * tgt_n
    local = es_ref.shape[1]
    lanes = nt // 128
    gene_count = genes_ref.shape[1]
    base = t * rows
    own = pl.ds(pl.multiple_of(base, 128), rows)

    def place(linear):
        return (linear // tgt_n, linear % tgt_n)

    planes = src_n // 4
    hops = sorted(
        (
            -min(dz, planes - dz) - dx - dy,
            (dz, dx, dc, dy),
        )
        for dz in range(planes) for dx in range(2) for dc in range(2) for dy in range(tgt_n)
        if dz + dx + dc + dy
    )

    def everyone(act):
        if n > 64:
            def one(k, carry):
                act(place((me + n // 2 + k) % n))
                return carry

            lax.fori_loop(0, n // 2, one, 0)
            lax.fori_loop(n // 2 + 1, n, one, 0)
            return
        for unused, (dz, dx, dc, dy) in hops:
            plane = s // 4 if dz == 0 else (s // 4 + dz) % planes
            column = s // 2 % 2 if dx == 0 else 1 - s // 2 % 2
            core_of = s % 2 if dc == 0 else 1 - s % 2
            act((plane * 4 + column * 2 + core_of, t if dy == 0 else (t + dy) % tgt_n))

    def owner(tile):
        if tile < 16:
            return (src_n // 2 - 4 + tile // 2, (tile % 2) * (tgt_n // 2))
        return (src_n // 2 + 4, 0)

    barrier = pltpu.get_barrier_semaphore()

    def greet(device):
        pl.semaphore_signal(
            barrier, inc=1, device_id=device, device_id_type=MESH
        )

    everyone(greet)

    plan_step = local // CHUNKS
    fetch_embed = pltpu.make_async_copy(es_ref, right.at[0:128], in_sem.at[0])
    fetch_plan = [
        pltpu.make_async_copy(
            plan_ref.at[c * plan_step:(c + 1) * plan_step],
            plan.at[c * plan_step:(c + 1) * plan_step], in_sem.at[3 + c],
        )
        for c in range(CHUNKS)
    ]
    fetch_expr = pltpu.make_async_copy(
        xs_ref.at[:, pl.ds(pl.multiple_of(base, 128), rows)], xs, in_sem.at[1]
    )
    fetch_genes = pltpu.make_async_copy(genes_ref, genes.at[t], in_sem.at[2])
    at_target = (pltpu.make_async_copy(et_ref, emb.at[t], in_sem.at[3 + CHUNKS]),
                 pltpu.make_async_copy(xt_ref, expr.at[t], in_sem.at[4 + CHUNKS]),
                 pltpu.make_async_copy(mt_ref, tmass.at[t], in_sem.at[5 + CHUNKS]))
    at_source = (pltpu.make_async_copy(ms_ref.at[:, own], masses_row, in_sem.at[6 + CHUNKS]),
                 pltpu.make_async_copy(fs_ref.at[:, own], potentials, in_sem.at[7 + CHUNKS]))
    for copy in (at_target[0], fetch_embed) + tuple(fetch_plan):
        copy.start()
    at_target[0].wait()
    target = emb[t]
    target_wide = target.astype(F32)
    q_tgt = [p.astype(F32) for p in split3(jnp.sum(target_wide * target_wide, axis=0, keepdims=True))]
    fetch_embed.wait()

    wide = right[0:128, :].astype(F32)
    q_src = [p.astype(F32) for p in split3(jnp.sum(wide * wide, axis=0, keepdims=True))]
    right[128:144, :] = rows_of(16, local, [1.0] + q_src).astype(BF16)

    here = 0.0
    for c in range(CHUNKS):
        fetch_plan[c].wait()
        at = slice(c * plan_step, (c + 1) * plan_step)
        here = here + dot(right[:, at], plan[at, :])
    for copy in at_target[1:] + at_source + (fetch_expr, fetch_genes):
        copy.start()
    by_e = here[0:128, :]
    by_one = here[128:129, :]
    by_q = here[129:130, :] + (here[130:131, :] + here[131:132, :])
    high, mid, low = split3(by_e)
    across_dims = ((1,), (1,))
    partial[0:16] = (
        dot(high, target, across_dims) + (dot(mid, target, across_dims) + dot(low, target, across_dims))
    ).reshape(16, 8, 128)
    ends = rows_of(16, cols, [1.0] + q_tgt).astype(BF16)
    ends = dot(ends, high, across_dims) + (dot(ends, mid, across_dims) + dot(ends, low, across_dims))
    q_wide = q_tgt[0] + (q_tgt[1] + q_tgt[2])
    row = lax.broadcasted_iota(jnp.int32, (8, 128), 0)
    edge_t = jnp.where(row == 0, ends[0:1, :], jnp.where(row == 1, ends[1:2, :] + (ends[2:3, :] + ends[3:4, :]), 0.0))
    sums = rows_of(8, cols, [0.0, 0.0, by_one, by_q])
    scalars = rows_of(8, cols, [0.0, 0.0, 0.0, 0.0, by_one, by_one * q_wide, by_q, by_q * q_wide])
    partial[16] = edge_t + dot3(sums, target, across_dims) + jnp.sum(scalars, axis=1, keepdims=True)

    pl.semaphore_wait(barrier, n - 1)

    def to_owner(tile):
        return pltpu.make_async_remote_copy(
            src_ref=partial.at[tile], dst_ref=collected.at[me],
            send_sem=rs_send.at[tile], recv_sem=rs_recv,
            device_id=owner(tile), device_id_type=MESH,
        )

    def mine(tile):
        return (s == owner(tile)[0]) & (t == owner(tile)[1])

    for tile in range(TILES):
        @pl.when(jnp.logical_not(mine(tile)))
        def _():
            to_owner(tile).start()

    half = s % 2
    sibling = (s + 1 - 2 * half, t)

    def part(size):
        return pl.ds(pl.multiple_of(half * (size // 2), size // 2), size // 2)

    emb_part, gene_part = part(128), part(cols)
    across, along = [], []
    for d in range(1, tgt_n):
        peer = (s, (t + d) % tgt_n)
        other = (t + tgt_n - d) % tgt_n
        for a, (ref, held, piece) in enumerate(
            ((emb.at[t], emb, emb_part), (expr.at[t], expr, emb_part), (genes.at[t], genes, gene_part))
        ):
            across.append(
                pltpu.make_async_remote_copy(
                    src_ref=ref.at[piece], dst_ref=held.at[t, piece],
                    send_sem=tgt_send.at[a, d - 1], recv_sem=tgt_recv.at[a, d - 1],
                    device_id=peer, device_id_type=MESH,
                )
            )
            along.append(
                pltpu.make_async_remote_copy(
                    src_ref=held.at[other, piece], dst_ref=held.at[other, piece],
                    send_sem=fw_send.at[a, d - 1], recv_sem=fw_recv.at[a, d - 1],
                    device_id=sibling, device_id_type=MESH,
                )
            )
    masses = [
        pltpu.make_async_remote_copy(
            src_ref=tmass.at[t], dst_ref=tmass.at[t],
            send_sem=tgt_send.at[3, d - 1], recv_sem=tgt_recv.at[3, d - 1],
            device_id=(s, (t + d) % tgt_n), device_id_type=MESH,
        )
        for d in range(1, tgt_n)
    ]
    for copy in at_target[1:] + (fetch_genes,):
        copy.wait()
    for copy in across[0::3] + across[1::3] + masses:
        copy.start()

    own_tile, owns = 0, False
    for tile in range(TILES):
        own_tile = jnp.where(mine(tile), tile, own_tile)
        owns = owns | mine(tile)

    @pl.when(owns)
    def _():
        collected[me] = partial[own_tile]
        whole = collected.at[pl.ds(0, n - 1)]
        pltpu.make_async_remote_copy(
            src_ref=whole, dst_ref=whole, send_sem=ag_send, recv_sem=rs_recv,
            device_id=place((me + 1) % n), device_id_type=MESH,
        ).wait_recv()
        core[own_tile] = jnp.sum(collected[...], axis=0)

        def spread(device):
            pltpu.make_async_remote_copy(
                src_ref=core.at[own_tile], dst_ref=core.at[own_tile],
                send_sem=ag_send, recv_sem=ag_recv.at[own_tile],
                device_id=device, device_id_type=MESH,
            ).start()

        everyone(spread)

    fetch_expr.wait()
    for copy in at_source:
        copy.wait()
    q_high, q_mid, q_low = [right[129 + k:130 + k, own].astype(F32) for k in range(3)]
    f_pieces = [p.astype(F32) for p in split3(0.5 * potentials[...])]
    m_pieces = [p.astype(F32) for p in split3(masses_row[...])]
    border[...] = jnp.zeros_like(border)
    border[0:16, :] = rows_of(
        16, rows, [q_high, q_high, q_high, q_mid, q_mid, q_low, 1.0, 1.0, 1.0] + f_pieces + m_pieces
    ).astype(BF16)
    pick = lax.broadcasted_iota(jnp.int32, (128, 128), 0)
    select = jnp.where((pick >= 12) & (pick < 15), 1.0, 0.0).astype(BF16)

    def turn_over(c, carry):
        at = pl.ds(pl.multiple_of(c * 128, 128), 128)
        e_rows = right[0:128, pl.ds(pl.multiple_of(base + c * 128, 128), 128)].T
        ends_rows = border[:, at].T
        lhs[at, 0:128] = xs[:, at].T
        lhs[at, 128:256] = e_rows
        lhs[at, 256:384] = e_rows
        lhs[at, 384:512] = ends_rows
        mass[at, :] = dot(ends_rows, select)
        return carry

    lax.fori_loop(0, rows // 128, turn_over, 0)

    for copy, onward in list(zip(across, along))[0::3] + list(zip(across, along))[1::3]:
        copy.wait_recv()
        onward.start()
    rhs[384:512, :] = jnp.zeros((128, nt), BF16)
    for copy in along[0::3] + along[1::3] + masses:
        copy.wait_recv()
    q_all = []
    for block in range(tgt_n):
        rhs[0:128, block * cols:(block + 1) * cols] = expr[block]
        e_wide = emb[block].astype(F32)
        q_all.append(jnp.sum(e_wide * e_wide, axis=0, keepdims=True))

    for tile in range(TILES):
        @pl.when(jnp.logical_not(mine(tile)))
        def _():
            pltpu.make_async_remote_copy(
                src_ref=core.at[tile], dst_ref=core.at[tile],
                send_sem=ag_send, recv_sem=ag_recv.at[tile],
                device_id=place((me + 1) % n), device_id_type=MESH,
            ).wait_recv()

    edge = core[16] * (1.0 / total_pairs)
    edge_cols = edge.T
    pieces = split3(core[...].reshape(TILES * 8, 128) * (1.0 / total_pairs))
    for block in range(tgt_n):
        at = slice(block * cols, (block + 1) * cols)
        e_t, q_t = emb[block], q_all[block]
        by_core = dot(pieces[0], e_t) + (dot(pieces[1], e_t) + dot(pieces[2], e_t))
        g_e = -2.0 * by_core[0:128, :] + edge_cols[:, 0:1] * q_t + edge_cols[:, 1:2]
        high, mid, unused = split3((-2.0 * GEOMETRY_WEIGHT) * g_e)
        rhs[128:256, at] = high
        rhs[256:384, at] = mid
        g_0 = -2.0 * by_core[130:131, :] + edge[4:5, 0:1] * q_t + edge[5:6, 0:1]
        g_1 = -2.0 * by_core[131:132, :] + edge[6:7, 0:1] * q_t + edge[7:8, 0:1]
        a_high, a_mid, a_low = [p.astype(F32) for p in split3(GEOMETRY_WEIGHT * g_0)]
        one_pieces = [p.astype(F32) for p in split3(GEOMETRY_WEIGHT * g_1)]
        rhs[384:400, at] = rows_of(
            16, cols, [a_high, a_mid, a_low, a_high, a_mid, a_high] + one_pieces + [1.0, 1.0, 1.0]
        ).astype(BF16)

    def share(turn, value):
        slots = logs.at[turn] if turn < PARTS else totals
        for c in range(value.shape[1] // 128):
            staged[c:c + 1, :] = value[:, c * 128:(c + 1) * 128]
        slots[me] = staged[0:value.shape[1] // 128, :].astype(slots.dtype)

        def send(device):
            pltpu.make_async_remote_copy(
                src_ref=slots.at[me], dst_ref=slots.at[me],
                send_sem=col_send.at[turn], recv_sem=col_recv.at[turn],
                device_id=device, device_id_type=MESH,
            ).start()

        everyone(send)
        whole = slots.at[pl.ds(0, n - 1)]
        every = pltpu.make_async_remote_copy(
            src_ref=whole, dst_ref=whole, send_sem=col_send.at[turn], recv_sem=col_recv.at[turn],
            device_id=place((me + 1) % n), device_id_type=MESH,
        )
        return every

    def scores(r, k):
        at, lane = slice(r * score_step, (r + 1) * score_step), slice(k * 256, (k + 1) * 256)
        tile = dot(lhs[at, :], rhs[:, lane]) * KAPPA
        score[at, lane] = tile
        return jnp.max(tile.reshape(score_step // 8, 8, 256), axis=0)

    def fold(r, k, top):
        at, lane = slice(r * score_step, (r + 1) * score_step), slice(k * 256, (k + 1) * 256)
        return jnp.sum(jnp.exp2(score[at, lane].reshape(score_step // 8, 8, 256) - top[None]), axis=0)

    def ended(k, top, total):
        whole = jnp.max(top, axis=0, keepdims=True)
        total = jnp.sum(total * jnp.exp2(top - whole), axis=0, keepdims=True)
        return whole + jnp.log2(total)

    blocks, tiles = rows // score_step, nt // 256
    done, last, first = [], None, []
    for k in range(tiles):
        top, total = -1e30, 0.0
        for r in range(blocks):
            top = jnp.maximum(top, scores(r, k))
            if k:
                total = total + fold(r, k - 1, last)
        if k:
            done.append(ended(k - 1, last, total))
            if k % (tiles // PARTS) == 0:
                first.append(share(k // (tiles // PARTS) - 1, jnp.concatenate(done[k - tiles // PARTS:], axis=1)))
        last = top
    total = 0.0
    for r in range(blocks):
        total = total + fold(r, tiles - 1, last)
    done.append(ended(tiles - 1, last, total))
    first.append(share(PARTS - 1, jnp.concatenate(done[len(done) - tiles // PARTS:], axis=1)))

    for copy in across[2::3]:
        copy.start()
    target_logs = jnp.log2(tmass[...].reshape(lanes, 128))
    some = lanes // PARTS
    sides = [slice(part_at * some * 128, (part_at + 1) * some * 128) for part_at in range(PARTS)]

    def potential(part_at):
        first[part_at].wait_recv()
        held = logs[part_at]
        top = jnp.max(held, axis=0)
        total = top + jnp.log2(jnp.sum(jnp.exp2(held - top[None]), axis=0))
        value = target_logs[part_at * some:(part_at + 1) * some, :] - total
        for c in range(some):
            gpot[0:1, (part_at * some + c) * 128:(part_at * some + c + 1) * 128] = value[c:c + 1, :]

    def spread_out(at, side):
        a = score[at, side] + gpot[0:1, side]
        top = jnp.max(a, axis=1, keepdims=True)
        p = jnp.exp2(a - top)
        prob[at, side] = p.astype(BF16)
        return top, p, jnp.sum(p, axis=1, keepdims=True)

    potential(0)
    for c in range(rows // middle_step):
        at = slice(c * middle_step, (c + 1) * middle_step)
        top, unused, total = spread_out(at, sides[0])
        factors[at, 0:128] = jnp.broadcast_to(top, (middle_step, 128))
        factors[at, 128:256] = jnp.broadcast_to(total, (middle_step, 128))
    potential(1)
    sums = [0.0, 0.0]
    for c in range(rows // middle_step):
        at = slice(c * middle_step, (c + 1) * middle_step)
        top, p, total = spread_out(at, sides[1])
        before = factors[at, 0:128]
        whole = jnp.maximum(before, top)
        scales = jnp.exp2(before - whole), jnp.exp2(top - whole)
        share_of = mass[at, :] / (scales[0] * factors[at, 128:256] + scales[1] * total)
        factors[at, 0:128] = scales[0]
        factors[at, 128:256] = scales[1]
        for k, (entries, scale) in enumerate(zip((prob[at, sides[0]].astype(F32), p), scales)):
            weight = jnp.concatenate([scale * share_of] * some, axis=1)
            sums[k] = sums[k] + jnp.sum((entries * weight).reshape(middle_step // 8, 8, some * 128), axis=0)
    second = share(PARTS, jnp.sum(jnp.concatenate(sums, axis=1), axis=0, keepdims=True))
    for copy, onward in list(zip(across, along))[2::3]:
        copy.wait_recv()
        onward.start()
    second.wait_recv()
    for copy in along[2::3]:
        copy.wait_recv()

    scaling = tmass[...].reshape(lanes, 128) / jnp.sum(totals[...].astype(F32), axis=0)
    columns = scaling.T
    for c in range(lanes):
        at = slice(c * 128, (c + 1) * 128)
        block, within = c * 128 // cols, c * 128 % cols
        scale_row[:, at] = jnp.broadcast_to(scaling[c:c + 1, :], (8, 128))
        weighted[at, :] = (genes[block, within:within + 128, :].astype(F32) * columns[:, c:c + 1]).astype(BF16)

    for copy in across + along + masses + first + [second]:
        copy.wait_send()
    for tile in range(TILES):
        @pl.when(jnp.logical_not(mine(tile)))
        def _():
            to_owner(tile).wait_send()

    @pl.when(owns)
    def _():
        whole = collected.at[pl.ds(0, n - 1)]
        pltpu.make_async_remote_copy(
            src_ref=whole, dst_ref=whole, send_sem=ag_send, recv_sem=rs_recv,
            device_id=place((me + 1) % n), device_id_type=MESH,
        ).wait_send()


def finish(prob_ref, weighted_ref, scale_ref, factors_ref, out_ref, held, sems, *, last_step):
    rows = prob_ref.shape[0]
    half = prob_ref.shape[1] // PARTS
    copies = []
    for c in range(rows // last_step):
        at = slice(c * last_step, (c + 1) * last_step)
        both, total = [], 0.0
        for k in range(PARTS):
            side = slice(k * half, (k + 1) * half)
            p, factor = prob_ref[at, side], factors_ref[at, k * 128:(k + 1) * 128]
            total = total + factor * jnp.sum(p.astype(F32) * scale_ref[0:1, side], axis=1, keepdims=True)
            both.append((dot(p, weighted_ref[side, :]), factor))
        inverse = 1.0 / total
        for g in range(held.shape[1] // 128):
            lane = slice(g * 128, (g + 1) * 128)
            held[at, lane] = sum(part[:, lane] * (factor * inverse) for part, factor in both).astype(BF16)
        copy = pltpu.make_async_copy(held.at[at], out_ref.at[at], sems.at[c])
        copy.start()
        copies.append(copy)
    for copy in copies:
        copy.wait()


def shards(src_n, tgt_n, es, et, xs, xt, plan, ms, mt, fs, genes):
    n = src_n * tgt_n
    local = es.shape[1]
    cols = et.shape[1]
    nt = cols * tgt_n
    rows = local // tgt_n
    total_pairs = float(local * src_n * nt)
    gene_count = genes.shape[1]
    score_step = min(rows, 512) if nt <= 1024 else 128
    middle_step = min(rows, 512) if nt <= 1024 else 64
    last_step = min(rows, 256)
    body = functools.partial(
        kernel, src_n, tgt_n, total_pairs, rows, score_step, middle_step
    )
    hbm = pl.BlockSpec(memory_space=pltpu.HBM)
    vmem = pl.BlockSpec(memory_space=pltpu.VMEM)
    dma = pltpu.SemaphoreType.DMA
    prob, weighted, scale_row, factors = pl.pallas_call(
        body,
        out_shape=[pltpu.VMEM((rows, nt), BF16), pltpu.VMEM((nt, gene_count), BF16), pltpu.VMEM((8, nt), F32), pltpu.VMEM((rows, 256), F32)],
        in_specs=[hbm] * 9,
        out_specs=[vmem] * 4,
        scratch_shapes=[
            pltpu.VMEM((144, local), BF16),
            pltpu.VMEM((local, cols), BF16),
            pltpu.VMEM((128, rows), BF16),
            pltpu.VMEM((1, rows), F32),
            pltpu.VMEM((1, rows), F32),
            pltpu.VMEM((tgt_n, 128, cols), BF16),
            pltpu.VMEM((tgt_n, 128, cols), BF16),
            pltpu.VMEM((tgt_n, cols // 128, 128), F32),
            pltpu.VMEM((tgt_n, cols, gene_count), BF16),
            pltpu.VMEM((TILES, 8, 128), F32),
            pltpu.VMEM((n, 8, 128), F32),
            pltpu.VMEM((TILES, 8, 128), F32),
            pltpu.VMEM((128, rows), BF16),
            pltpu.VMEM((rows, 512), BF16),
            pltpu.VMEM((rows, 128), F32),
            pltpu.VMEM((512, nt), BF16),
            pltpu.VMEM((rows, nt), F32),
            pltpu.VMEM((PARTS, n, nt // 128 // PARTS, 128), F32),
            pltpu.VMEM((n, nt // 128, 128), BF16),
            pltpu.VMEM((nt // 128, 128), F32),
            pltpu.VMEM((1, nt), F32),
            dma((8 + CHUNKS,)),
            dma((4, tgt_n - 1)),
            dma((4, tgt_n - 1)),
            dma((3, tgt_n - 1)),
            dma((3, tgt_n - 1)),
            dma((TILES,)),
            dma,
            dma,
            dma((TILES,)),
            dma((PARTS + 1,)),
            dma((PARTS + 1,)),
        ],
        compiler_params=pltpu.CompilerParams(
            collective_id=0, has_side_effects=True, vmem_limit_bytes=40 * 1024 * 1024
        ),
    )(*[
        pltpu.with_memory_space_constraint(value, pltpu.HBM)
        for value in (
            es, et, xs, xt, plan,
            ms.reshape(1, local), mt.reshape(cols // 128, 128), fs.reshape(1, local), genes,
        )
    ])
    return pl.pallas_call(
        functools.partial(finish, last_step=last_step),
        out_shape=jax.ShapeDtypeStruct((rows, gene_count), BF16),
        in_specs=[vmem] * 4,
        out_specs=hbm,
        scratch_shapes=[pltpu.VMEM((rows, gene_count), BF16), dma((rows // last_step,))],
        compiler_params=pltpu.CompilerParams(vmem_limit_bytes=16 * 1024 * 1024),
    )(
        pltpu.with_memory_space_constraint(prob, pltpu.VMEM),
        pltpu.with_memory_space_constraint(weighted, pltpu.VMEM),
        pltpu.with_memory_space_constraint(scale_row, pltpu.VMEM),
        pltpu.with_memory_space_constraint(factors, pltpu.VMEM),
    )


def solution(mesh):
    src_n = mesh.shape["src"]
    tgt_n = mesh.shape["tgt"]
    return jax.shard_map(
        functools.partial(shards, src_n, tgt_n),
        mesh=mesh,
        in_specs=(
            P(None, "src"),
            P(None, "tgt"),
            P(None, "src"),
            P(None, "tgt"),
            P("src", "tgt"),
            P("src"),
            P("tgt"),
            P("src"),
            P("tgt", None),
        ),
        out_specs=P(("src", "tgt"), None),
        check_vma=False,
    )
```

```python
import functools
import math

import jax
import jax.numpy as jnp
from jax import lax
from jax.experimental import pallas as pl
from jax.experimental.pallas import tpu as pltpu
from jax.sharding import PartitionSpec as P

EPSILON = 0.05
GEOMETRY_WEIGHT = 4.0
LOG2E = math.log2(math.e)
KAPPA = 2.0 * LOG2E / EPSILON
MESH = pl.DeviceIdType.MESH
F32 = jnp.float32
BF16 = jnp.bfloat16
TILES = 17
CHUNKS = 4
PARTS = 2
EDGE_WITH = 10


def split3(value):
    high = value.astype(BF16)
    rest = value - high.astype(F32)
    middle = rest.astype(BF16)
    low = (rest - middle.astype(F32)).astype(BF16)
    return high, middle, low


def dot(a, b, dims=((1,), (0,))):
    return lax.dot_general(a, b, (dims, ((), ())), preferred_element_type=F32)


def dot3(a, b, dims=((1,), (0,))):
    high, middle, low = split3(a)
    return dot(high, b, dims) + (dot(middle, b, dims) + dot(low, b, dims))


def rows_of(count, width, values):
    row = lax.broadcasted_iota(jnp.int32, (count, width), 0)
    held = jnp.zeros((count, width), F32)
    for k, value in enumerate(values):
        held = jnp.where(row == k, value, held)
    return held


def kernel(
    src_n, tgt_n, total_pairs, rows, score_step, middle_step,
    es_ref, et_ref, xs_ref, xt_ref, plan_ref, ms_ref, mt_ref, fs_ref, genes_ref,
    prob, weighted, scale_row, factors,
    right, plan, xs, masses_row, potentials, emb, expr, tmass, genes, partial, collected, edges, core,
    border, lhs, mass, rhs, score, logs, totals, staged, gpot,
    in_sem, tgt_send, tgt_recv, fw_send, fw_recv, rs_send, rs_recv, ag_send, ag_recv,
    col_send, col_recv, edge_send, edge_recv,
):
    n = src_n * tgt_n
    s = lax.axis_index("src")
    t = lax.axis_index("tgt")
    me = s * tgt_n + t
    cols = et_ref.shape[1]
    nt = cols * tgt_n
    local = es_ref.shape[1]
    lanes = nt // 128
    gene_count = genes_ref.shape[1]
    base = t * rows
    own = pl.ds(pl.multiple_of(base, 128), rows)

    def place(linear):
        return (linear // tgt_n, linear % tgt_n)

    planes = src_n // 4
    hops = sorted(
        (
            -min(dz, planes - dz) - dx - dy,
            (dz, dx, dc, dy),
        )
        for dz in range(planes) for dx in range(2) for dc in range(2) for dy in range(tgt_n)
        if dz + dx + dc + dy
    )

    def everyone(act):
        if n > 64:
            def one(k, carry):
                act(place((me + n // 2 + k) % n))
                return carry

            lax.fori_loop(0, n // 2, one, 0)
            lax.fori_loop(n // 2 + 1, n, one, 0)
            return
        for unused, (dz, dx, dc, dy) in hops:
            plane = s // 4 if dz == 0 else (s // 4 + dz) % planes
            column = s // 2 % 2 if dx == 0 else 1 - s // 2 % 2
            core_of = s % 2 if dc == 0 else 1 - s % 2
            act((plane * 4 + column * 2 + core_of, t if dy == 0 else (t + dy) % tgt_n))

    def owner(tile):
        if tile < 16:
            return (src_n // 2 - 4 + tile // 2, (tile % 2) * (tgt_n // 2))
        return owner(EDGE_WITH)

    barrier = pltpu.get_barrier_semaphore()

    def greet(device):
        pl.semaphore_signal(
            barrier, inc=1, device_id=device, device_id_type=MESH
        )

    everyone(greet)

    plan_step = local // CHUNKS
    fetch_embed = pltpu.make_async_copy(es_ref, right.at[0:128], in_sem.at[0])
    fetch_plan = [
        pltpu.make_async_copy(
            plan_ref.at[c * plan_step:(c + 1) * plan_step],
            plan.at[c * plan_step:(c + 1) * plan_step], in_sem.at[3 + c],
        )
        for c in range(CHUNKS)
    ]
    fetch_expr = pltpu.make_async_copy(
        xs_ref.at[:, pl.ds(pl.multiple_of(base, 128), rows)], xs, in_sem.at[1]
    )
    fetch_genes = pltpu.make_async_copy(genes_ref, genes.at[t], in_sem.at[2])
    at_target = (pltpu.make_async_copy(et_ref, emb.at[t], in_sem.at[3 + CHUNKS]),
                 pltpu.make_async_copy(xt_ref, expr.at[t], in_sem.at[4 + CHUNKS]),
                 pltpu.make_async_copy(mt_ref, tmass.at[t], in_sem.at[5 + CHUNKS]))
    at_source = (pltpu.make_async_copy(ms_ref.at[:, own], masses_row, in_sem.at[6 + CHUNKS]),
                 pltpu.make_async_copy(fs_ref.at[:, own], potentials, in_sem.at[7 + CHUNKS]))
    for copy in (at_target[0], fetch_embed) + tuple(fetch_plan):
        copy.start()
    at_target[0].wait()
    target = emb[t]
    target_wide = target.astype(F32)
    q_tgt = [p.astype(F32) for p in split3(jnp.sum(target_wide * target_wide, axis=0, keepdims=True))]
    fetch_embed.wait()

    wide = right[0:128, :].astype(F32)
    q_src = [p.astype(F32) for p in split3(jnp.sum(wide * wide, axis=0, keepdims=True))]
    right[128:144, :] = rows_of(16, local, [1.0] + q_src).astype(BF16)

    here = 0.0
    for c in range(CHUNKS):
        fetch_plan[c].wait()
        at = slice(c * plan_step, (c + 1) * plan_step)
        here = here + dot(right[:, at], plan[at, :])
    for copy in at_target[1:] + at_source + (fetch_expr, fetch_genes):
        copy.start()
    by_e = here[0:128, :]
    by_one = here[128:129, :]
    by_q = here[129:130, :] + (here[130:131, :] + here[131:132, :])
    high, mid, low = split3(by_e)
    across_dims = ((1,), (1,))
    partial[0:16] = (
        dot(high, target, across_dims) + (dot(mid, target, across_dims) + dot(low, target, across_dims))
    ).reshape(16, 8, 128)
    ends = rows_of(16, cols, [1.0] + q_tgt).astype(BF16)
    ends = dot(ends, high, across_dims) + (dot(ends, mid, across_dims) + dot(ends, low, across_dims))
    q_wide = q_tgt[0] + (q_tgt[1] + q_tgt[2])
    row = lax.broadcasted_iota(jnp.int32, (8, 128), 0)
    edge_t = jnp.where(row == 0, ends[0:1, :], jnp.where(row == 1, ends[1:2, :] + (ends[2:3, :] + ends[3:4, :]), 0.0))
    sums = rows_of(8, cols, [0.0, 0.0, by_one, by_q])
    scalars = rows_of(8, cols, [0.0, 0.0, 0.0, 0.0, by_one, by_one * q_wide, by_q, by_q * q_wide])
    partial[16] = edge_t + dot3(sums, target, across_dims) + jnp.sum(scalars, axis=1, keepdims=True)

    pl.semaphore_wait(barrier, n - 1)

    def to_owner(tile):
        return pltpu.make_async_remote_copy(
            src_ref=partial.at[tile], dst_ref=(edges if tile == 16 else collected).at[me],
            send_sem=rs_send.at[tile], recv_sem=edge_recv if tile == 16 else rs_recv,
            device_id=owner(tile), device_id_type=MESH,
        )

    def mine(tile):
        return (s == owner(tile)[0]) & (t == owner(tile)[1])

    for tile in range(TILES):
        @pl.when(jnp.logical_not(mine(tile)))
        def _():
            to_owner(tile).start()

    half = s % 2
    sibling = (s + 1 - 2 * half, t)

    def part(size):
        return pl.ds(pl.multiple_of(half * (size // 2), size // 2), size // 2)

    emb_part, gene_part = part(128), part(cols)
    across, along = [], []
    for d in range(1, tgt_n):
        peer = (s, (t + d) % tgt_n)
        other = (t + tgt_n - d) % tgt_n
        for a, (ref, held, piece) in enumerate(
            ((emb.at[t], emb, emb_part), (expr.at[t], expr, emb_part), (genes.at[t], genes, gene_part))
        ):
            across.append(
                pltpu.make_async_remote_copy(
                    src_ref=ref.at[piece], dst_ref=held.at[t, piece],
                    send_sem=tgt_send.at[a, d - 1], recv_sem=tgt_recv.at[a, d - 1],
                    device_id=peer, device_id_type=MESH,
                )
            )
            along.append(
                pltpu.make_async_remote_copy(
                    src_ref=held.at[other, piece], dst_ref=held.at[other, piece],
                    send_sem=fw_send.at[a, d - 1], recv_sem=fw_recv.at[a, d - 1],
                    device_id=sibling, device_id_type=MESH,
                )
            )
    masses = [
        pltpu.make_async_remote_copy(
            src_ref=tmass.at[t], dst_ref=tmass.at[t],
            send_sem=tgt_send.at[3, d - 1], recv_sem=tgt_recv.at[3, d - 1],
            device_id=(s, (t + d) % tgt_n), device_id_type=MESH,
        )
        for d in range(1, tgt_n)
    ]
    for copy in at_target[1:] + (fetch_genes,):
        copy.wait()
    for copy in across[0::3] + across[1::3] + masses:
        copy.start()

    own_tile, owns = 0, False
    for tile in range(16):
        own_tile = jnp.where(mine(tile), tile, own_tile)
        owns = owns | mine(tile)

    @pl.when(owns)
    def _():
        collected[me] = partial[own_tile]
        whole = collected.at[pl.ds(0, n - 1)]
        pltpu.make_async_remote_copy(
            src_ref=whole, dst_ref=whole, send_sem=ag_send, recv_sem=rs_recv,
            device_id=place((me + 1) % n), device_id_type=MESH,
        ).wait_recv()
        core[own_tile] = jnp.sum(collected[...], axis=0)

        def spread(device):
            pltpu.make_async_remote_copy(
                src_ref=core.at[own_tile], dst_ref=core.at[own_tile],
                send_sem=ag_send, recv_sem=ag_recv.at[own_tile],
                device_id=device, device_id_type=MESH,
            ).start()

        everyone(spread)

    @pl.when(mine(16))
    def _():
        edges[me] = partial[16]
        whole = edges.at[pl.ds(0, n - 1)]
        pltpu.make_async_remote_copy(
            src_ref=whole, dst_ref=whole, send_sem=edge_send, recv_sem=edge_recv,
            device_id=place((me + 1) % n), device_id_type=MESH,
        ).wait_recv()
        core[16] = jnp.sum(edges[...], axis=0)

        def spread_edge(device):
            pltpu.make_async_remote_copy(
                src_ref=core.at[16], dst_ref=core.at[16],
                send_sem=edge_send, recv_sem=ag_recv.at[16],
                device_id=device, device_id_type=MESH,
            ).start()

        everyone(spread_edge)

    fetch_expr.wait()
    for copy in at_source:
        copy.wait()
    q_high, q_mid, q_low = [right[129 + k:130 + k, own].astype(F32) for k in range(3)]
    f_pieces = [p.astype(F32) for p in split3(0.5 * potentials[...])]
    m_pieces = [p.astype(F32) for p in split3(masses_row[...])]
    border[...] = jnp.zeros_like(border)
    border[0:16, :] = rows_of(
        16, rows, [q_high, q_high, q_high, q_mid, q_mid, q_low, 1.0, 1.0, 1.0] + f_pieces + m_pieces
    ).astype(BF16)
    pick = lax.broadcasted_iota(jnp.int32, (128, 128), 0)
    select = jnp.where((pick >= 12) & (pick < 15), 1.0, 0.0).astype(BF16)

    def turn_over(c, carry):
        at = pl.ds(pl.multiple_of(c * 128, 128), 128)
        e_rows = right[0:128, pl.ds(pl.multiple_of(base + c * 128, 128), 128)].T
        ends_rows = border[:, at].T
        lhs[at, 0:128] = xs[:, at].T
        lhs[at, 128:256] = e_rows
        lhs[at, 256:384] = e_rows
        lhs[at, 384:512] = ends_rows
        mass[at, :] = dot(ends_rows, select)
        return carry

    lax.fori_loop(0, rows // 128, turn_over, 0)

    for copy, onward in list(zip(across, along))[0::3] + list(zip(across, along))[1::3]:
        copy.wait_recv()
        onward.start()
    rhs[384:512, :] = jnp.zeros((128, nt), BF16)
    for copy in along[0::3] + along[1::3] + masses:
        copy.wait_recv()
    q_all = []
    for block in range(tgt_n):
        rhs[0:128, block * cols:(block + 1) * cols] = expr[block]
        e_wide = emb[block].astype(F32)
        q_all.append(jnp.sum(e_wide * e_wide, axis=0, keepdims=True))

    for tile in range(TILES):
        @pl.when(jnp.logical_not(mine(tile)))
        def _():
            pltpu.make_async_remote_copy(
                src_ref=core.at[tile], dst_ref=core.at[tile],
                send_sem=ag_send, recv_sem=ag_recv.at[tile],
                device_id=place((me + 1) % n), device_id_type=MESH,
            ).wait_recv()

    edge = core[16] * (1.0 / total_pairs)
    edge_cols = edge.T
    pieces = split3(core[...].reshape(TILES * 8, 128) * (1.0 / total_pairs))
    for block in range(tgt_n):
        at = slice(block * cols, (block + 1) * cols)
        e_t, q_t = emb[block], q_all[block]
        by_core = dot(pieces[0], e_t) + (dot(pieces[1], e_t) + dot(pieces[2], e_t))
        g_e = -2.0 * by_core[0:128, :] + edge_cols[:, 0:1] * q_t + edge_cols[:, 1:2]
        high, mid, unused = split3((-2.0 * GEOMETRY_WEIGHT) * g_e)
        rhs[128:256, at] = high
        rhs[256:384, at] = mid
        g_0 = -2.0 * by_core[130:131, :] + edge[4:5, 0:1] * q_t + edge[5:6, 0:1]
        g_1 = -2.0 * by_core[131:132, :] + edge[6:7, 0:1] * q_t + edge[7:8, 0:1]
        a_high, a_mid, a_low = [p.astype(F32) for p in split3(GEOMETRY_WEIGHT * g_0)]
        one_pieces = [p.astype(F32) for p in split3(GEOMETRY_WEIGHT * g_1)]
        rhs[384:400, at] = rows_of(
            16, cols, [a_high, a_mid, a_low, a_high, a_mid, a_high] + one_pieces + [1.0, 1.0, 1.0]
        ).astype(BF16)

    def share(turn, value):
        slots = logs.at[turn] if turn < PARTS else totals
        for c in range(value.shape[1] // 128):
            staged[c:c + 1, :] = value[:, c * 128:(c + 1) * 128]
        slots[me] = staged[0:value.shape[1] // 128, :].astype(slots.dtype)

        def send(device):
            pltpu.make_async_remote_copy(
                src_ref=slots.at[me], dst_ref=slots.at[me],
                send_sem=col_send.at[turn], recv_sem=col_recv.at[turn],
                device_id=device, device_id_type=MESH,
            ).start()

        everyone(send)
        whole = slots.at[pl.ds(0, n - 1)]
        every = pltpu.make_async_remote_copy(
            src_ref=whole, dst_ref=whole, send_sem=col_send.at[turn], recv_sem=col_recv.at[turn],
            device_id=place((me + 1) % n), device_id_type=MESH,
        )
        return every

    def scores(r, k):
        at, lane = slice(r * score_step, (r + 1) * score_step), slice(k * 256, (k + 1) * 256)
        tile = dot(lhs[at, :], rhs[:, lane]) * KAPPA
        score[at, lane] = tile
        return jnp.max(tile.reshape(score_step // 8, 8, 256), axis=0)

    def fold(r, k, top):
        at, lane = slice(r * score_step, (r + 1) * score_step), slice(k * 256, (k + 1) * 256)
        return jnp.sum(jnp.exp2(score[at, lane].reshape(score_step // 8, 8, 256) - top[None]), axis=0)

    def ended(k, top, total):
        whole = jnp.max(top, axis=0, keepdims=True)
        total = jnp.sum(total * jnp.exp2(top - whole), axis=0, keepdims=True)
        return whole + jnp.log2(total)

    blocks, tiles = rows // score_step, nt // 256
    done, last, first = [], None, []
    for k in range(tiles):
        top, total = -1e30, 0.0
        for r in range(blocks):
            top = jnp.maximum(top, scores(r, k))
            if k:
                total = total + fold(r, k - 1, last)
        if k:
            done.append(ended(k - 1, last, total))
            if k % (tiles // PARTS) == 0:
                first.append(share(k // (tiles // PARTS) - 1, jnp.concatenate(done[k - tiles // PARTS:], axis=1)))
        last = top
    total = 0.0
    for r in range(blocks):
        total = total + fold(r, tiles - 1, last)
    done.append(ended(tiles - 1, last, total))
    first.append(share(PARTS - 1, jnp.concatenate(done[len(done) - tiles // PARTS:], axis=1)))

    for copy in across[2::3]:
        copy.start()
    target_logs = jnp.log2(tmass[...].reshape(lanes, 128))
    some = lanes // PARTS
    sides = [slice(part_at * some * 128, (part_at + 1) * some * 128) for part_at in range(PARTS)]

    def potential(part_at):
        first[part_at].wait_recv()
        held = logs[part_at]
        top = jnp.max(held, axis=0)
        total = top + jnp.log2(jnp.sum(jnp.exp2(held - top[None]), axis=0))
        value = target_logs[part_at * some:(part_at + 1) * some, :] - total
        for c in range(some):
            gpot[0:1, (part_at * some + c) * 128:(part_at * some + c + 1) * 128] = value[c:c + 1, :]

    def spread_out(at, side):
        a = score[at, side] + gpot[0:1, side]
        top = jnp.max(a, axis=1, keepdims=True)
        p = jnp.exp2(a - top)
        prob[at, side] = p.astype(BF16)
        return top, p, jnp.sum(p, axis=1, keepdims=True)

    potential(0)
    for c in range(rows // middle_step):
        at = slice(c * middle_step, (c + 1) * middle_step)
        top, unused, total = spread_out(at, sides[0])
        factors[at, 0:128] = jnp.broadcast_to(top, (middle_step, 128))
        factors[at, 128:256] = jnp.broadcast_to(total, (middle_step, 128))
    potential(1)
    sums = [0.0, 0.0]
    for c in range(rows // middle_step):
        at = slice(c * middle_step, (c + 1) * middle_step)
        top, p, total = spread_out(at, sides[1])
        before = factors[at, 0:128]
        whole = jnp.maximum(before, top)
        scales = jnp.exp2(before - whole), jnp.exp2(top - whole)
        share_of = mass[at, :] / (scales[0] * factors[at, 128:256] + scales[1] * total)
        factors[at, 0:128] = scales[0]
        factors[at, 128:256] = scales[1]
        for k, (entries, scale) in enumerate(zip((prob[at, sides[0]].astype(F32), p), scales)):
            weight = jnp.concatenate([scale * share_of] * some, axis=1)
            sums[k] = sums[k] + jnp.sum((entries * weight).reshape(middle_step // 8, 8, some * 128), axis=0)
    second = share(PARTS, jnp.sum(jnp.concatenate(sums, axis=1), axis=0, keepdims=True))
    for copy, onward in list(zip(across, along))[2::3]:
        copy.wait_recv()
        onward.start()
    second.wait_recv()
    for copy in along[2::3]:
        copy.wait_recv()

    scaling = tmass[...].reshape(lanes, 128) / jnp.sum(totals[...].astype(F32), axis=0)
    columns = scaling.T
    for c in range(lanes):
        at = slice(c * 128, (c + 1) * 128)
        block, within = c * 128 // cols, c * 128 % cols
        scale_row[:, at] = jnp.broadcast_to(scaling[c:c + 1, :], (8, 128))
        weighted[at, :] = (genes[block, within:within + 128, :].astype(F32) * columns[:, c:c + 1]).astype(BF16)

    for copy in across + along + masses + first + [second]:
        copy.wait_send()
    for tile in range(TILES):
        @pl.when(jnp.logical_not(mine(tile)))
        def _():
            to_owner(tile).wait_send()

    @pl.when(owns)
    def _():
        whole = collected.at[pl.ds(0, n - 1)]
        pltpu.make_async_remote_copy(
            src_ref=whole, dst_ref=whole, send_sem=ag_send, recv_sem=rs_recv,
            device_id=place((me + 1) % n), device_id_type=MESH,
        ).wait_send()

    @pl.when(mine(16))
    def _():
        whole = edges.at[pl.ds(0, n - 1)]
        pltpu.make_async_remote_copy(
            src_ref=whole, dst_ref=whole, send_sem=edge_send, recv_sem=edge_recv,
            device_id=place((me + 1) % n), device_id_type=MESH,
        ).wait_send()


def finish(prob_ref, weighted_ref, scale_ref, factors_ref, out_ref, held, sems, *, last_step):
    rows = prob_ref.shape[0]
    half = prob_ref.shape[1] // PARTS
    copies = []
    sizes = [last_step] * (rows // last_step - 1) + [last_step // 2, last_step // 4, last_step // 4]
    for c, size in enumerate(sizes):
        at = slice(sum(sizes[:c]), sum(sizes[:c]) + size)
        both, total = [], 0.0
        for k in range(PARTS):
            side = slice(k * half, (k + 1) * half)
            p, factor = prob_ref[at, side], factors_ref[at, k * 128:(k + 1) * 128]
            total = total + factor * jnp.sum(p.astype(F32) * scale_ref[0:1, side], axis=1, keepdims=True)
            both.append((dot(p, weighted_ref[side, :]), factor))
        inverse = 1.0 / total
        for g in range(held.shape[1] // 128):
            lane = slice(g * 128, (g + 1) * 128)
            held[at, lane] = sum(part[:, lane] * (factor * inverse) for part, factor in both).astype(BF16)
        copy = pltpu.make_async_copy(held.at[at], out_ref.at[at], sems.at[c])
        copy.start()
        copies.append(copy)
    for copy in copies:
        copy.wait()


def shards(src_n, tgt_n, es, et, xs, xt, plan, ms, mt, fs, genes):
    n = src_n * tgt_n
    local = es.shape[1]
    cols = et.shape[1]
    nt = cols * tgt_n
    rows = local // tgt_n
    total_pairs = float(local * src_n * nt)
    gene_count = genes.shape[1]
    score_step = min(rows, 512) if nt <= 1024 else 128
    middle_step = min(rows, 512) if nt <= 1024 else 64
    last_step = min(rows, 512)
    body = functools.partial(
        kernel, src_n, tgt_n, total_pairs, rows, score_step, middle_step
    )
    hbm = pl.BlockSpec(memory_space=pltpu.HBM)
    vmem = pl.BlockSpec(memory_space=pltpu.VMEM)
    dma = pltpu.SemaphoreType.DMA
    prob, weighted, scale_row, factors = pl.pallas_call(
        body,
        out_shape=[pltpu.VMEM((rows, nt), BF16), pltpu.VMEM((nt, gene_count), BF16), pltpu.VMEM((8, nt), F32), pltpu.VMEM((rows, 256), F32)],
        in_specs=[hbm] * 9,
        out_specs=[vmem] * 4,
        scratch_shapes=[
            pltpu.VMEM((144, local), BF16),
            pltpu.VMEM((local, cols), BF16),
            pltpu.VMEM((128, rows), BF16),
            pltpu.VMEM((1, rows), F32),
            pltpu.VMEM((1, rows), F32),
            pltpu.VMEM((tgt_n, 128, cols), BF16),
            pltpu.VMEM((tgt_n, 128, cols), BF16),
            pltpu.VMEM((tgt_n, cols // 128, 128), F32),
            pltpu.VMEM((tgt_n, cols, gene_count), BF16),
            pltpu.VMEM((TILES, 8, 128), F32),
            pltpu.VMEM((n, 8, 128), F32),
            pltpu.VMEM((n, 8, 128), F32),
            pltpu.VMEM((TILES, 8, 128), F32),
            pltpu.VMEM((128, rows), BF16),
            pltpu.VMEM((rows, 512), BF16),
            pltpu.VMEM((rows, 128), F32),
            pltpu.VMEM((512, nt), BF16),
            pltpu.VMEM((rows, nt), F32),
            pltpu.VMEM((PARTS, n, nt // 128 // PARTS, 128), F32),
            pltpu.VMEM((n, nt // 128, 128), BF16),
            pltpu.VMEM((nt // 128, 128), F32),
            pltpu.VMEM((1, nt), F32),
            dma((8 + CHUNKS,)),
            dma((4, tgt_n - 1)),
            dma((4, tgt_n - 1)),
            dma((3, tgt_n - 1)),
            dma((3, tgt_n - 1)),
            dma((TILES,)),
            dma,
            dma,
            dma((TILES,)),
            dma((PARTS + 1,)),
            dma((PARTS + 1,)),
            dma,
            dma,
        ],
        compiler_params=pltpu.CompilerParams(
            collective_id=0, has_side_effects=True, vmem_limit_bytes=40 * 1024 * 1024
        ),
    )(*[
        pltpu.with_memory_space_constraint(value, pltpu.HBM)
        for value in (
            es, et, xs, xt, plan,
            ms.reshape(1, local), mt.reshape(cols // 128, 128), fs.reshape(1, local), genes,
        )
    ])
    return pl.pallas_call(
        functools.partial(finish, last_step=last_step),
        out_shape=jax.ShapeDtypeStruct((rows, gene_count), BF16),
        in_specs=[vmem] * 4,
        out_specs=hbm,
        scratch_shapes=[pltpu.VMEM((rows, gene_count), BF16), dma((rows // last_step + 2,))],
        compiler_params=pltpu.CompilerParams(vmem_limit_bytes=16 * 1024 * 1024),
    )(
        pltpu.with_memory_space_constraint(prob, pltpu.VMEM),
        pltpu.with_memory_space_constraint(weighted, pltpu.VMEM),
        pltpu.with_memory_space_constraint(scale_row, pltpu.VMEM),
        pltpu.with_memory_space_constraint(factors, pltpu.VMEM),
    )


def solution(mesh):
    src_n = mesh.shape["src"]
    tgt_n = mesh.shape["tgt"]
    return jax.shard_map(
        functools.partial(shards, src_n, tgt_n),
        mesh=mesh,
        in_specs=(
            P(None, "src"),
            P(None, "tgt"),
            P(None, "src"),
            P(None, "tgt"),
            P("src", "tgt"),
            P("src"),
            P("tgt"),
            P("src"),
            P("tgt", None),
        ),
        out_specs=P(("src", "tgt"), None),
        check_vma=False,
    )
```

```python
import functools
import math

import jax
import jax.numpy as jnp
from jax import lax
from jax.experimental import pallas as pl
from jax.experimental.pallas import tpu as pltpu
from jax.sharding import PartitionSpec as P

EPSILON = 0.05
GEOMETRY_WEIGHT = 4.0
LOG2E = math.log2(math.e)
KAPPA = 2.0 * LOG2E / EPSILON
MESH = pl.DeviceIdType.MESH
F32 = jnp.float32
BF16 = jnp.bfloat16
TILES = 17
CHUNKS = 4
PARTS = 2
EDGE_WITH = 10


def split3(value):
    high = value.astype(BF16)
    rest = value - high.astype(F32)
    middle = rest.astype(BF16)
    low = (rest - middle.astype(F32)).astype(BF16)
    return high, middle, low


def dot(a, b, dims=((1,), (0,))):
    return lax.dot_general(a, b, (dims, ((), ())), preferred_element_type=F32)


def dot3(a, b, dims=((1,), (0,))):
    high, middle, low = split3(a)
    return dot(high, b, dims) + (dot(middle, b, dims) + dot(low, b, dims))


def rows_of(count, width, values):
    row = lax.broadcasted_iota(jnp.int32, (count, width), 0)
    held = jnp.zeros((count, width), F32)
    for k, value in enumerate(values):
        held = jnp.where(row == k, value, held)
    return held


def kernel(
    src_n, tgt_n, total_pairs, rows, score_step, middle_step,
    es_ref, et_ref, xs_ref, xt_ref, plan_ref, ms_ref, mt_ref, fs_ref, genes_ref,
    prob, weighted, scale_row, factors,
    right, plan, xs, masses_row, potentials, emb, expr, tmass, genes, partial, collected, edges, core,
    border, lhs, mass, rhs, score, logs, totals, staged, gpot,
    in_sem, tgt_send, tgt_recv, fw_send, fw_recv, rs_send, rs_recv, ag_send, ag_recv,
    col_send, col_recv, edge_send, edge_recv,
):
    n = src_n * tgt_n
    s = lax.axis_index("src")
    t = lax.axis_index("tgt")
    me = s * tgt_n + t
    cols = et_ref.shape[1]
    nt = cols * tgt_n
    local = es_ref.shape[1]
    lanes = nt // 128
    gene_count = genes_ref.shape[1]
    base = t * rows
    own = pl.ds(pl.multiple_of(base, 128), rows)

    def place(linear):
        return (linear // tgt_n, linear % tgt_n)

    planes = src_n // 4
    hops = sorted(
        (
            -min(dz, planes - dz) - dx - dy,
            (dz, dx, dc, dy),
        )
        for dz in range(planes) for dx in range(2) for dc in range(2) for dy in range(tgt_n)
        if dz + dx + dc + dy
    )

    def everyone(act):
        if n > 64:
            def one(k, carry):
                act(place((me + n // 2 + k) % n))
                return carry

            lax.fori_loop(0, n // 2, one, 0)
            lax.fori_loop(n // 2 + 1, n, one, 0)
            return
        for unused, (dz, dx, dc, dy) in hops:
            plane = s // 4 if dz == 0 else (s // 4 + dz) % planes
            column = s // 2 % 2 if dx == 0 else 1 - s // 2 % 2
            core_of = s % 2 if dc == 0 else 1 - s % 2
            act((plane * 4 + column * 2 + core_of, t if dy == 0 else (t + dy) % tgt_n))

    def owner(tile):
        if tile < 16:
            return (src_n // 2 - 4 + tile // 2, (tile % 2) * (tgt_n // 2))
        return owner(EDGE_WITH)

    barrier = pltpu.get_barrier_semaphore()

    def greet(device):
        pl.semaphore_signal(
            barrier, inc=1, device_id=device, device_id_type=MESH
        )

    everyone(greet)

    plan_step = local // CHUNKS
    fetch_embed = pltpu.make_async_copy(es_ref, right.at[0:128], in_sem.at[0])
    fetch_plan = [
        pltpu.make_async_copy(
            plan_ref.at[c * plan_step:(c + 1) * plan_step],
            plan.at[c * plan_step:(c + 1) * plan_step], in_sem.at[3 + c],
        )
        for c in range(CHUNKS)
    ]
    fetch_expr = pltpu.make_async_copy(
        xs_ref.at[:, pl.ds(pl.multiple_of(base, 128), rows)], xs, in_sem.at[1]
    )
    fetch_genes = pltpu.make_async_copy(genes_ref, genes.at[t], in_sem.at[2])
    at_target = (pltpu.make_async_copy(et_ref, emb.at[t], in_sem.at[3 + CHUNKS]),
                 pltpu.make_async_copy(xt_ref, expr.at[t], in_sem.at[4 + CHUNKS]),
                 pltpu.make_async_copy(mt_ref, tmass.at[t], in_sem.at[5 + CHUNKS]))
    at_source = (pltpu.make_async_copy(ms_ref.at[:, own], masses_row, in_sem.at[6 + CHUNKS]),
                 pltpu.make_async_copy(fs_ref.at[:, own], potentials, in_sem.at[7 + CHUNKS]))
    for copy in (at_target[0], fetch_embed) + tuple(fetch_plan):
        copy.start()
    at_target[0].wait()
    target = emb[t]
    target_wide = target.astype(F32)
    q_tgt = [p.astype(F32) for p in split3(jnp.sum(target_wide * target_wide, axis=0, keepdims=True))]
    fetch_embed.wait()

    wide = right[0:128, :].astype(F32)
    q_src = [p.astype(F32) for p in split3(jnp.sum(wide * wide, axis=0, keepdims=True))]
    right[128:144, :] = rows_of(16, local, [1.0] + q_src).astype(BF16)

    here = 0.0
    for c in range(CHUNKS):
        fetch_plan[c].wait()
        at = slice(c * plan_step, (c + 1) * plan_step)
        here = here + dot(right[:, at], plan[at, :])
    for copy in at_target[1:] + at_source + (fetch_expr, fetch_genes):
        copy.start()
    by_e = here[0:128, :]
    by_one = here[128:129, :]
    by_q = here[129:130, :] + (here[130:131, :] + here[131:132, :])
    high, mid, low = split3(by_e)
    across_dims = ((1,), (1,))
    partial[0:16] = (
        dot(high, target, across_dims) + (dot(mid, target, across_dims) + dot(low, target, across_dims))
    ).reshape(16, 8, 128)
    ends = rows_of(16, cols, [1.0] + q_tgt).astype(BF16)
    ends = dot(ends, high, across_dims) + (dot(ends, mid, across_dims) + dot(ends, low, across_dims))
    q_wide = q_tgt[0] + (q_tgt[1] + q_tgt[2])
    row = lax.broadcasted_iota(jnp.int32, (8, 128), 0)
    edge_t = jnp.where(row == 0, ends[0:1, :], jnp.where(row == 1, ends[1:2, :] + (ends[2:3, :] + ends[3:4, :]), 0.0))
    sums = rows_of(8, cols, [0.0, 0.0, by_one, by_q])
    scalars = rows_of(8, cols, [0.0, 0.0, 0.0, 0.0, by_one, by_one * q_wide, by_q, by_q * q_wide])
    partial[16] = edge_t + dot3(sums, target, across_dims) + jnp.sum(scalars, axis=1, keepdims=True)

    pl.semaphore_wait(barrier, n - 1)

    def to_owner(tile):
        return pltpu.make_async_remote_copy(
            src_ref=partial.at[tile], dst_ref=(edges if tile == 16 else collected).at[me],
            send_sem=rs_send.at[tile], recv_sem=edge_recv if tile == 16 else rs_recv,
            device_id=owner(tile), device_id_type=MESH,
        )

    def mine(tile):
        return (s == owner(tile)[0]) & (t == owner(tile)[1])

    for tile in range(TILES):
        @pl.when(jnp.logical_not(mine(tile)))
        def _():
            to_owner(tile).start()

    half = s % 2
    sibling = (s + 1 - 2 * half, t)

    def part(size):
        return pl.ds(pl.multiple_of(half * (size // 2), size // 2), size // 2)

    emb_part, gene_part = part(128), part(cols)
    across, along = [], []
    for d in range(1, tgt_n):
        peer = (s, (t + d) % tgt_n)
        other = (t + tgt_n - d) % tgt_n
        for a, (ref, held, piece) in enumerate(
            ((emb.at[t], emb, emb_part), (expr.at[t], expr, emb_part), (genes.at[t], genes, gene_part))
        ):
            across.append(
                pltpu.make_async_remote_copy(
                    src_ref=ref.at[piece], dst_ref=held.at[t, piece],
                    send_sem=tgt_send.at[a, d - 1], recv_sem=tgt_recv.at[a, d - 1],
                    device_id=peer, device_id_type=MESH,
                )
            )
            along.append(
                pltpu.make_async_remote_copy(
                    src_ref=held.at[other, piece], dst_ref=held.at[other, piece],
                    send_sem=fw_send.at[a, d - 1], recv_sem=fw_recv.at[a, d - 1],
                    device_id=sibling, device_id_type=MESH,
                )
            )
    masses = [
        pltpu.make_async_remote_copy(
            src_ref=tmass.at[t], dst_ref=tmass.at[t],
            send_sem=tgt_send.at[3, d - 1], recv_sem=tgt_recv.at[3, d - 1],
            device_id=(s, (t + d) % tgt_n), device_id_type=MESH,
        )
        for d in range(1, tgt_n)
    ]
    for copy in at_target[1:] + (fetch_genes,):
        copy.wait()
    for copy in across[0::3] + across[1::3] + masses:
        copy.start()

    own_tile, owns = 0, False
    for tile in range(16):
        own_tile = jnp.where(mine(tile), tile, own_tile)
        owns = owns | mine(tile)

    @pl.when(owns)
    def _():
        collected[me] = partial[own_tile]
        whole = collected.at[pl.ds(0, n - 1)]
        pltpu.make_async_remote_copy(
            src_ref=whole, dst_ref=whole, send_sem=ag_send, recv_sem=rs_recv,
            device_id=place((me + 1) % n), device_id_type=MESH,
        ).wait_recv()
        core[own_tile] = jnp.sum(collected[...], axis=0)

        def spread(device):
            pltpu.make_async_remote_copy(
                src_ref=core.at[own_tile], dst_ref=core.at[own_tile],
                send_sem=ag_send, recv_sem=ag_recv.at[own_tile],
                device_id=device, device_id_type=MESH,
            ).start()

        everyone(spread)

    @pl.when(mine(16))
    def _():
        edges[me] = partial[16]
        whole = edges.at[pl.ds(0, n - 1)]
        pltpu.make_async_remote_copy(
            src_ref=whole, dst_ref=whole, send_sem=edge_send, recv_sem=edge_recv,
            device_id=place((me + 1) % n), device_id_type=MESH,
        ).wait_recv()
        core[16] = jnp.sum(edges[...], axis=0)

        def spread_edge(device):
            pltpu.make_async_remote_copy(
                src_ref=core.at[16], dst_ref=core.at[16],
                send_sem=edge_send, recv_sem=ag_recv.at[16],
                device_id=device, device_id_type=MESH,
            ).start()

        everyone(spread_edge)

    fetch_expr.wait()
    for copy in at_source:
        copy.wait()
    q_high, q_mid, q_low = [right[129 + k:130 + k, own].astype(F32) for k in range(3)]
    f_pieces = [p.astype(F32) for p in split3(0.5 * potentials[...])]
    m_pieces = [p.astype(F32) for p in split3(masses_row[...])]
    border[...] = jnp.zeros_like(border)
    border[0:16, :] = rows_of(
        16, rows, [q_high, q_high, q_high, q_mid, q_mid, q_low, 1.0, 1.0, 1.0] + f_pieces + m_pieces
    ).astype(BF16)
    pick = lax.broadcasted_iota(jnp.int32, (128, 128), 0)
    select = jnp.where((pick >= 12) & (pick < 15), 1.0, 0.0).astype(BF16)

    def turn_over(c, carry):
        at = pl.ds(pl.multiple_of(c * 128, 128), 128)
        e_rows = right[0:128, pl.ds(pl.multiple_of(base + c * 128, 128), 128)].T
        ends_rows = border[:, at].T
        lhs[at, 0:128] = xs[:, at].T
        lhs[at, 128:256] = e_rows
        lhs[at, 256:384] = e_rows
        lhs[at, 384:512] = ends_rows
        mass[at, :] = dot(ends_rows, select)
        return carry

    lax.fori_loop(0, rows // 128, turn_over, 0)

    for copy, onward in list(zip(across, along))[0::3] + list(zip(across, along))[1::3]:
        copy.wait_recv()
        onward.start()
    rhs[384:512, :] = jnp.zeros((128, nt), BF16)
    for copy in along[0::3] + along[1::3] + masses:
        copy.wait_recv()
    q_all = []
    for block in range(tgt_n):
        rhs[0:128, block * cols:(block + 1) * cols] = expr[block]
        e_wide = emb[block].astype(F32)
        q_all.append(jnp.sum(e_wide * e_wide, axis=0, keepdims=True))

    for tile in range(TILES):
        @pl.when(jnp.logical_not(mine(tile)))
        def _():
            pltpu.make_async_remote_copy(
                src_ref=core.at[tile], dst_ref=core.at[tile],
                send_sem=ag_send, recv_sem=ag_recv.at[tile],
                device_id=place((me + 1) % n), device_id_type=MESH,
            ).wait_recv()

    edge = core[16] * (1.0 / total_pairs)
    edge_cols = edge.T
    pieces = split3(core[...].reshape(TILES * 8, 128) * (1.0 / total_pairs))
    for block in range(tgt_n):
        at = slice(block * cols, (block + 1) * cols)
        e_t, q_t = emb[block], q_all[block]
        by_core = dot(pieces[0], e_t) + (dot(pieces[1], e_t) + dot(pieces[2], e_t))
        g_e = -2.0 * by_core[0:128, :] + edge_cols[:, 0:1] * q_t + edge_cols[:, 1:2]
        high, mid, unused = split3((-2.0 * GEOMETRY_WEIGHT) * g_e)
        rhs[128:256, at] = high
        rhs[256:384, at] = mid
        g_0 = -2.0 * by_core[130:131, :] + edge[4:5, 0:1] * q_t + edge[5:6, 0:1]
        g_1 = -2.0 * by_core[131:132, :] + edge[6:7, 0:1] * q_t + edge[7:8, 0:1]
        a_high, a_mid, a_low = [p.astype(F32) for p in split3(GEOMETRY_WEIGHT * g_0)]
        one_pieces = [p.astype(F32) for p in split3(GEOMETRY_WEIGHT * g_1)]
        rhs[384:400, at] = rows_of(
            16, cols, [a_high, a_mid, a_low, a_high, a_mid, a_high] + one_pieces + [1.0, 1.0, 1.0]
        ).astype(BF16)

    def share(turn, value):
        slots = logs.at[turn] if turn < PARTS else totals
        for c in range(value.shape[1] // 128):
            staged[c:c + 1, :] = value[:, c * 128:(c + 1) * 128]
        slots[me] = staged[0:value.shape[1] // 128, :].astype(slots.dtype)

        def send(device):
            pltpu.make_async_remote_copy(
                src_ref=slots.at[me], dst_ref=slots.at[me],
                send_sem=col_send.at[turn], recv_sem=col_recv.at[turn],
                device_id=device, device_id_type=MESH,
            ).start()

        everyone(send)
        whole = slots.at[pl.ds(0, n - 1)]
        every = pltpu.make_async_remote_copy(
            src_ref=whole, dst_ref=whole, send_sem=col_send.at[turn], recv_sem=col_recv.at[turn],
            device_id=place((me + 1) % n), device_id_type=MESH,
        )
        return every

    def scores(r, k):
        at, lane = slice(r * score_step, (r + 1) * score_step), slice(k * 256, (k + 1) * 256)
        tile = dot(lhs[at, :], rhs[:, lane]) * KAPPA
        score[at, lane] = tile
        return jnp.max(tile.reshape(score_step // 8, 8, 256), axis=0)

    def fold(r, k, block_top, top, total):
        at, lane = slice(r * score_step, (r + 1) * score_step), slice(k * 256, (k + 1) * 256)
        now = block_top if r == 0 else jnp.maximum(top, block_top)
        here = jnp.sum(jnp.exp2(score[at, lane].reshape(score_step // 8, 8, 256) - now[None]), axis=0)
        return now, here if r == 0 else total * jnp.exp2(top - now) + here

    def ended(k, top, total):
        whole = jnp.max(top, axis=0, keepdims=True)
        total = jnp.sum(total * jnp.exp2(top - whole), axis=0, keepdims=True)
        return whole + jnp.log2(total)

    blocks, tiles = rows // score_step, nt // 256
    done, first, waiting, top, total = [], [], None, None, None
    for step in range(blocks * tiles + 1):
        at = (step % blocks, step // blocks)
        block_top = scores(*at) if step < blocks * tiles else None
        if waiting:
            (r, k), held_top = waiting
            top, total = fold(r, k, held_top, top, total)
            if r == blocks - 1:
                done.append(ended(k, top, total))
                if len(done) % (tiles // PARTS) == 0:
                    first.append(share(len(first), jnp.concatenate(done[-(tiles // PARTS):], axis=1)))
        waiting = (at, block_top)
    for copy in across[2::3]:
        copy.start()
    target_logs = jnp.log2(tmass[...].reshape(lanes, 128))
    some = lanes // PARTS
    sides = [slice(part_at * some * 128, (part_at + 1) * some * 128) for part_at in range(PARTS)]

    def potential(part_at):
        first[part_at].wait_recv()
        held = logs[part_at]
        top = jnp.max(held, axis=0)
        total = top + jnp.log2(jnp.sum(jnp.exp2(held - top[None]), axis=0))
        value = target_logs[part_at * some:(part_at + 1) * some, :] - total
        for c in range(some):
            gpot[0:1, (part_at * some + c) * 128:(part_at * some + c + 1) * 128] = value[c:c + 1, :]

    def spread_out(at, side):
        a = score[at, side] + gpot[0:1, side]
        top = jnp.max(a, axis=1, keepdims=True)
        p = jnp.exp2(a - top)
        prob[at, side] = p.astype(BF16)
        return top, p, jnp.sum(p, axis=1, keepdims=True)

    potential(0)
    for c in range(rows // middle_step):
        at = slice(c * middle_step, (c + 1) * middle_step)
        top, unused, total = spread_out(at, sides[0])
        factors[at, 0:128] = jnp.broadcast_to(top, (middle_step, 128))
        factors[at, 128:256] = jnp.broadcast_to(total, (middle_step, 128))
    potential(1)
    sums = [0.0, 0.0]
    for c in range(rows // middle_step):
        at = slice(c * middle_step, (c + 1) * middle_step)
        top, p, total = spread_out(at, sides[1])
        before = factors[at, 0:128]
        whole = jnp.maximum(before, top)
        scales = jnp.exp2(before - whole), jnp.exp2(top - whole)
        share_of = mass[at, :] / (scales[0] * factors[at, 128:256] + scales[1] * total)
        factors[at, 0:128] = scales[0]
        factors[at, 128:256] = scales[1]
        for k, (entries, scale) in enumerate(zip((prob[at, sides[0]].astype(F32), p), scales)):
            weight = jnp.concatenate([scale * share_of] * some, axis=1)
            sums[k] = sums[k] + jnp.sum((entries * weight).reshape(middle_step // 8, 8, some * 128), axis=0)
    second = share(PARTS, jnp.sum(jnp.concatenate(sums, axis=1), axis=0, keepdims=True))
    for copy, onward in list(zip(across, along))[2::3]:
        copy.wait_recv()
        onward.start()
    second.wait_recv()
    for copy in along[2::3]:
        copy.wait_recv()

    scaling = tmass[...].reshape(lanes, 128) / jnp.sum(totals[...].astype(F32), axis=0)
    columns = scaling.T
    for c in range(lanes):
        at = slice(c * 128, (c + 1) * 128)
        block, within = c * 128 // cols, c * 128 % cols
        scale_row[:, at] = jnp.broadcast_to(scaling[c:c + 1, :], (8, 128))
        weighted[at, :] = (genes[block, within:within + 128, :].astype(F32) * columns[:, c:c + 1]).astype(BF16)

    for copy in across + along + masses + first + [second]:
        copy.wait_send()
    for tile in range(TILES):
        @pl.when(jnp.logical_not(mine(tile)))
        def _():
            to_owner(tile).wait_send()

    @pl.when(owns)
    def _():
        whole = collected.at[pl.ds(0, n - 1)]
        pltpu.make_async_remote_copy(
            src_ref=whole, dst_ref=whole, send_sem=ag_send, recv_sem=rs_recv,
            device_id=place((me + 1) % n), device_id_type=MESH,
        ).wait_send()

    @pl.when(mine(16))
    def _():
        whole = edges.at[pl.ds(0, n - 1)]
        pltpu.make_async_remote_copy(
            src_ref=whole, dst_ref=whole, send_sem=edge_send, recv_sem=edge_recv,
            device_id=place((me + 1) % n), device_id_type=MESH,
        ).wait_send()


def finish(prob_ref, weighted_ref, scale_ref, factors_ref, out_ref, held, sems, *, last_step):
    rows = prob_ref.shape[0]
    half = prob_ref.shape[1] // PARTS
    copies = []
    sizes = [last_step] * (rows // last_step - 1) + [last_step // 2, last_step // 4, last_step // 4]
    for c, size in enumerate(sizes):
        at = slice(sum(sizes[:c]), sum(sizes[:c]) + size)
        both, total = [], 0.0
        for k in range(PARTS):
            side = slice(k * half, (k + 1) * half)
            p, factor = prob_ref[at, side], factors_ref[at, k * 128:(k + 1) * 128]
            total = total + factor * jnp.sum(p.astype(F32) * scale_ref[0:1, side], axis=1, keepdims=True)
            both.append((dot(p, weighted_ref[side, :]), factor))
        inverse = 1.0 / total
        for g in range(held.shape[1] // 128):
            lane = slice(g * 128, (g + 1) * 128)
            held[at, lane] = sum(part[:, lane] * (factor * inverse) for part, factor in both).astype(BF16)
        copy = pltpu.make_async_copy(held.at[at], out_ref.at[at], sems.at[c])
        copy.start()
        copies.append(copy)
    for copy in copies:
        copy.wait()


def shards(src_n, tgt_n, es, et, xs, xt, plan, ms, mt, fs, genes):
    n = src_n * tgt_n
    local = es.shape[1]
    cols = et.shape[1]
    nt = cols * tgt_n
    rows = local // tgt_n
    total_pairs = float(local * src_n * nt)
    gene_count = genes.shape[1]
    score_step = min(rows, 256) if nt <= 1024 else 128
    middle_step = min(rows, 512) if nt <= 1024 else 64
    last_step = min(rows, 512)
    body = functools.partial(
        kernel, src_n, tgt_n, total_pairs, rows, score_step, middle_step
    )
    hbm = pl.BlockSpec(memory_space=pltpu.HBM)
    vmem = pl.BlockSpec(memory_space=pltpu.VMEM)
    dma = pltpu.SemaphoreType.DMA
    prob, weighted, scale_row, factors = pl.pallas_call(
        body,
        out_shape=[pltpu.VMEM((rows, nt), BF16), pltpu.VMEM((nt, gene_count), BF16), pltpu.VMEM((8, nt), F32), pltpu.VMEM((rows, 256), F32)],
        in_specs=[hbm] * 9,
        out_specs=[vmem] * 4,
        scratch_shapes=[
            pltpu.VMEM((144, local), BF16),
            pltpu.VMEM((local, cols), BF16),
            pltpu.VMEM((128, rows), BF16),
            pltpu.VMEM((1, rows), F32),
            pltpu.VMEM((1, rows), F32),
            pltpu.VMEM((tgt_n, 128, cols), BF16),
            pltpu.VMEM((tgt_n, 128, cols), BF16),
            pltpu.VMEM((tgt_n, cols // 128, 128), F32),
            pltpu.VMEM((tgt_n, cols, gene_count), BF16),
            pltpu.VMEM((TILES, 8, 128), F32),
            pltpu.VMEM((n, 8, 128), F32),
            pltpu.VMEM((n, 8, 128), F32),
            pltpu.VMEM((TILES, 8, 128), F32),
            pltpu.VMEM((128, rows), BF16),
            pltpu.VMEM((rows, 512), BF16),
            pltpu.VMEM((rows, 128), F32),
            pltpu.VMEM((512, nt), BF16),
            pltpu.VMEM((rows, nt), F32),
            pltpu.VMEM((PARTS, n, nt // 128 // PARTS, 128), F32),
            pltpu.VMEM((n, nt // 128, 128), BF16),
            pltpu.VMEM((nt // 128, 128), F32),
            pltpu.VMEM((1, nt), F32),
            dma((8 + CHUNKS,)),
            dma((4, tgt_n - 1)),
            dma((4, tgt_n - 1)),
            dma((3, tgt_n - 1)),
            dma((3, tgt_n - 1)),
            dma((TILES,)),
            dma,
            dma,
            dma((TILES,)),
            dma((PARTS + 1,)),
            dma((PARTS + 1,)),
            dma,
            dma,
        ],
        compiler_params=pltpu.CompilerParams(
            collective_id=0, has_side_effects=True, vmem_limit_bytes=40 * 1024 * 1024
        ),
    )(*[
        pltpu.with_memory_space_constraint(value, pltpu.HBM)
        for value in (
            es, et, xs, xt, plan,
            ms.reshape(1, local), mt.reshape(cols // 128, 128), fs.reshape(1, local), genes,
        )
    ])
    return pl.pallas_call(
        functools.partial(finish, last_step=last_step),
        out_shape=jax.ShapeDtypeStruct((rows, gene_count), BF16),
        in_specs=[vmem] * 4,
        out_specs=hbm,
        scratch_shapes=[pltpu.VMEM((rows, gene_count), BF16), dma((rows // last_step + 2,))],
        compiler_params=pltpu.CompilerParams(vmem_limit_bytes=16 * 1024 * 1024),
    )(
        pltpu.with_memory_space_constraint(prob, pltpu.VMEM),
        pltpu.with_memory_space_constraint(weighted, pltpu.VMEM),
        pltpu.with_memory_space_constraint(scale_row, pltpu.VMEM),
        pltpu.with_memory_space_constraint(factors, pltpu.VMEM),
    )


def solution(mesh):
    src_n = mesh.shape["src"]
    tgt_n = mesh.shape["tgt"]
    return jax.shard_map(
        functools.partial(shards, src_n, tgt_n),
        mesh=mesh,
        in_specs=(
            P(None, "src"),
            P(None, "tgt"),
            P(None, "src"),
            P(None, "tgt"),
            P("src", "tgt"),
            P("src"),
            P("tgt"),
            P("src"),
            P("tgt", None),
        ),
        out_specs=P(("src", "tgt"), None),
        check_vma=False,
    )
```
